128 devices in a mesh: dp: 4 (over z), cell: 32 (over x, y, core).
Axes of the slice: x: 4, y: 4, z: 4, core: 2. Of those that a mesh axis runs over, the one named last changes fastest.
Arguments:
- vectors: bfloat16 [4, 12288, 64, 128], P('dp', 'cell'), may hold values from -120 to 120
- block_cells: int32 [4, 12288], P('dp', 'cell'), may hold values from 0 to 30
- dest_counts: int32 [4, 32, 32], P('dp', 'cell'), may hold values from 0 to 24, as said below
Outputs:
- cell_mean: float32 [1024, 128], P('cell')
- cell_cov: float32 [1024, 128, 128], P('cell')
The draws below stay inside these ranges and needn't reach their ends.
Inputs may be any that keep to these rules, and one draw needn't show every extreme that they name: Each device's dest_counts sum to 384; in each group one owner receives exactly 24 blocks from every device of the group, and every device sends no block to one other owner.
All inputs are finite; a program needn't handle non-finite values.
Results may differ from the reference program's by a relative error of at most 0.0003.
Values may be sent and summed in bfloat16 or wider, within the bound.
No kernel may reach another device: no remote copies, remote signals or barrier semaphores. Data moves between devices by JAX's collectives and lax.ppermute only.
A program may use at most 128 MiB of HBM per device.

```python
import math
import jax
import jax.numpy as jnp
from jax import lax

D = 128
CELLS = 1024
BLOCK = 64
BLK_DEV = 384
BLOCKS = 12288
CELL_DEV = 32
N_DP = 4
N_CELL = 32


def draw_vectors(key, part):
    keys = jax.random.split(key, 5)
    shape = (N_DP, BLOCKS, BLOCK, D)
    base = jnp.clip(jax.random.normal(keys[0], shape, jnp.float32), -5.0, 5.0)
    offset = jax.random.uniform(keys[1], (D,), jnp.float32, -1.0, 1.0)
    block_scale = jnp.exp(jax.random.uniform(keys[2], (N_DP, BLOCKS), jnp.float32, jnp.log(0.4), jnp.log(4.0)))
    mixing = jax.random.uniform(keys[3], (3, D), jnp.float32, -0.6, 0.6)
    mixed = base + mixing[0] * jnp.roll(base, 1, axis=3) + mixing[1] * jnp.roll(base, 5, axis=3) + mixing[2] * jnp.roll(base, 17, axis=3)
    column_scale = jnp.exp(jax.random.uniform(keys[4], (D,), jnp.float32, jnp.log(0.5), jnp.log(2.0)))
    return (block_scale[:, :, None, None] * column_scale * mixed + offset).astype(jnp.bfloat16)


def one_order(order_key):
    return jax.random.permutation(order_key, N_CELL)


def draw_dest_counts(key, part):
    average = BLK_DEV // N_CELL
    hot_key, cold_key, order_key, size_key = jax.random.split(key, 4)
    hot_owner = jax.random.randint(hot_key, (N_DP, 1), 0, N_CELL)
    cold_owner = (hot_owner + 1 + jax.random.randint(cold_key, (N_DP, N_CELL), 0, N_CELL - 1)) % N_CELL
    order_keys = jax.random.split(order_key, N_DP * N_CELL)
    orders = jax.vmap(one_order)(order_keys).reshape(N_DP, N_CELL, N_CELL)
    is_other = (orders != hot_owner[:, :, None]) & (orders != cold_owner[:, :, None])
    rank_of = jnp.cumsum(is_other.astype(jnp.int32), axis=2) - 1
    pair_sizes = jax.random.randint(size_key, (N_DP, N_CELL, N_CELL // 2), 0, average + 1)
    pair_index = jnp.clip(rank_of // 2, 0, N_CELL // 2 - 1)
    sizes_at = jnp.take_along_axis(pair_sizes, pair_index, axis=2)
    signs = jnp.where(rank_of % 2 == 0, 1, -1)
    amount_at = jnp.where(is_other, average + signs * sizes_at, 0)
    owners = jnp.arange(N_CELL, dtype=jnp.int32)
    counts = jnp.sum((orders[:, :, :, None] == owners[None, None, None, :]).astype(jnp.int32) * amount_at[:, :, :, None], axis=2)
    counts = jnp.where(owners[None, None, :] == hot_owner[:, :, None], 2 * average, counts)
    return counts.astype(jnp.int32)


def set_ends(values, own_key, least, largest):
    shape = values.shape
    place = [jax.random.randint(jax.random.fold_in(own_key, axis), (), 0, shape[axis]) for axis in range(len(shape))]
    values = values.at[tuple(place)].set(least)
    longest = shape.index(max(shape))
    place[longest] = (place[longest] + 1) % shape[longest]
    return values.at[tuple(place)].set(largest)


def setup_inputs(seed: int = 0) -> dict:
    seeds = jax.random.split(jax.random.key(seed), 4)
    return {
        "vectors": draw_vectors(jax.random.fold_in(seeds[3], 71), 0),
        "block_cells": set_ends(jax.random.randint(seeds[1], (N_DP, BLOCKS), 0, CELL_DEV - 1), jax.random.fold_in(seeds[1], 1), 0, (CELL_DEV - 1) - 1).astype(jnp.int32),
        "dest_counts": draw_dest_counts(jax.random.fold_in(seeds[3], 71), 0),
    }


def chan_update(left, right):
    left_count, left_mean, left_scatter = left
    right_count, right_mean, right_scatter = right
    total_count = left_count + right_count
    safe_count = jnp.maximum(total_count, 1.0)
    difference = right_mean - left_mean
    average = left_mean + difference * (right_count / safe_count)[:, None]
    weight = left_count * right_count / safe_count
    scatter = left_scatter + right_scatter + weight[:, None, None] * difference[:, :, None] * difference[:, None, :]
    return (total_count, average, scatter)


def group_moments(group_rows, cell_list):
    batch_size = math.gcd(BLOCKS, 512)
    def accumulate(running, batch_item):
        rows_in, cells_in = batch_item
        as_float = rows_in.astype(jnp.float32)
        gram_blocks = jnp.einsum("brd,bre->bde", as_float, as_float, precision=lax.Precision.HIGHEST).reshape(batch_size, D * D)
        row_sums = jnp.sum(as_float, axis=1)
        block_rows = jnp.full((batch_size,), float(BLOCK), dtype=jnp.float32)
        return (running[0] + jax.ops.segment_sum(block_rows, cells_in, num_segments=CELLS),
                running[1] + jax.ops.segment_sum(row_sums, cells_in, num_segments=CELLS),
                running[2] + jax.ops.segment_sum(gram_blocks, cells_in, num_segments=CELLS)), None
    initial = (jnp.zeros((CELLS,), jnp.float32), jnp.zeros((CELLS, D), jnp.float32), jnp.zeros((CELLS, D * D), jnp.float32))
    items = (group_rows.reshape(BLOCKS // batch_size, batch_size, BLOCK, D), cell_list.reshape(BLOCKS // batch_size, batch_size))
    result, _ = lax.scan(accumulate, initial, items)
    return result


def reference(vectors, block_cells, dest_counts):
    count_ends = jnp.cumsum(dest_counts, axis=2)
    places = jnp.arange(BLK_DEV, dtype=jnp.int32)
    owner_index = jnp.sum((count_ends[:, :, None, :] <= places[None, None, :, None]).astype(jnp.int32), axis=3)
    global_cell = (owner_index * CELL_DEV + block_cells.reshape(N_DP, N_CELL, BLK_DEV)).astype(jnp.int32).reshape(N_DP, BLOCKS)
    merged = None
    for group_index in range(N_DP):
        counts, sums, grams = group_moments(vectors[group_index], global_cell[group_index])
        average = sums / jnp.maximum(counts, 1.0)[:, None]
        scatter = grams.reshape(CELLS, D, D) - counts[:, None, None] * average[:, :, None] * average[:, None, :]
        current = (counts, average, scatter)
        merged = current if merged is None else chan_update(merged, current)
    total_count, average, scatter = merged
    return average, scatter / jnp.maximum(total_count, 1.0)[:, None, None]
```

```python
import jax
import jax.numpy as jnp
from jax import lax
from jax.experimental import pallas as pl
from jax.experimental.pallas import tpu as pltpu
from jax.sharding import PartitionSpec as P

CELLS = 1024
NX = NY = NZ = 4
NC = 2
OWNERS = NX * NY * NC
CELL_DEV = CELLS // OWNERS
BLK = 384
ROWS = 64
D = 128
RUN = 12
SLOTS = 4 * RUN
SHIFTS = [(d, dc) for d in (0, 1, 3, 2) for dc in (0, 1)]
GROUPS = len(SHIFTS)
TRASH = 4 * CELL_DEV
LIST = 400
PAIR = 8
F32 = jnp.float32
I32 = jnp.int32
PACKED = CELL_DEV * ROWS
PIECE = PACKED + 3 * CELL_DEV
QCELL = CELL_DEV // NZ
QPACKED = QCELL * ROWS
QPIECE = QPACKED + 3 * QCELL
VMEM_LIMIT = 48 * 1024 * 1024


def at(x, y, c):
    return (x * NY + y) * NC + c


def cell_perm(dx, dy, dc):
    return [
        (at(x, y, c), at((x + dx) % NX, (y + dy) % NY, c ^ dc))
        for x in range(NX)
        for y in range(NY)
        for c in range(NC)
    ]


def dp_perm(dz):
    return [(z, (z + dz) % NZ) for z in range(NZ)]


def place():
    me = lax.axis_index("cell")
    return me // (NY * NC), (me // NC) % NY, me % NC


def other_core(c, dc):
    return (c + dc) % NC


def run_bounds(count, offset, half):
    first = (count + 1) // 2
    n = first if half == 0 else count - first
    start = offset if half == 0 else offset + first
    return n, start, jnp.minimum(start, BLK - RUN)


def pack_body(pos, counts, vectors, *refs):
    outs = refs[: 2 * GROUPS]
    offsets, sems = refs[2 * GROUPS :]
    x, y, c = pos[0], pos[1], pos[2]
    total = jnp.int32(0)
    for o in range(OWNERS):
        offsets[o] = total
        total = total + counts[o]
    copies = []
    for half in (0, 1):
        for g, (d, dc) in enumerate(SHIFTS):
            oc = other_core(c, dc)
            for k in range(4):
                o = at((x + d) % NX, k, oc) if half == 0 else at(k, (y + d) % NY, oc)
                _, _, start = run_bounds(counts[o], offsets[o], half)
                copies.append(
                    pltpu.make_async_copy(
                        vectors.at[pl.ds(start, RUN)],
                        outs[half * GROUPS + g].at[pl.ds(k * RUN, RUN)],
                        sems.at[(half * GROUPS + g) * 4 + k],
                    )
                )
                copies[-1].start()
    for copy in copies:
        copy.wait()


def pack(pos, counts, vectors):
    shape = jax.ShapeDtypeStruct((SLOTS, ROWS, D), vectors.dtype)
    return pl.pallas_call(
        pack_body,
        out_shape=[shape] * (2 * GROUPS),
        in_specs=[
            pl.BlockSpec(memory_space=pltpu.SMEM),
            pl.BlockSpec(memory_space=pltpu.SMEM),
            pl.BlockSpec(memory_space=pl.ANY),
        ],
        out_specs=[pl.BlockSpec(memory_space=pl.ANY)] * (2 * GROUPS),
        scratch_shapes=[pltpu.SMEM((OWNERS,), I32), pltpu.SemaphoreType.DMA((2 * GROUPS * 4,))],
        name="pack",
    )(pos, counts, vectors)


def lists_body(pos, meta, lists, sizes, tallies):
    x, y, c = pos[0], pos[1], pos[2]

    def clear(i, _):
        tallies[i] = jnp.int32(0)
        return 0

    lax.fori_loop(0, 2 * TRASH, clear, 0)

    def prefix(s, _):
        def step(o, total):
            count = meta[s, BLK + o]
            meta_next = total + count
            lists[2 * LIST + s * OWNERS + o] = total
            return meta_next

        lax.fori_loop(0, OWNERS, step, jnp.int32(0))
        return 0

    lax.fori_loop(0, OWNERS, prefix, 0)
    for half in (0, 1):
        filled = jnp.int32(0)
        for g, (d, dc) in enumerate(SHIFTS):
            sc = other_core(c, dc)
            s = at((x + NX - d) % NX, y, sc) if half == 0 else at(x, (y + NY - d) % NY, sc)
            for k in range(4):
                o = at(x, k, c) if half == 0 else at(k, y, c)
                n, start, copied = run_bounds(meta[s, BLK + o], lists[2 * LIST + s * OWNERS + o], half)
                slot = (g * 4 + k) * RUN + start - copied
                piece = lax.rem(k + 4 - (y if half == 0 else x), 4)

                def add(j, f, s=s, start=start, slot=slot, piece=piece, half=half):
                    cell = piece * CELL_DEV + meta[s, start + j]
                    lists[half * LIST + f] = (slot + j) * 256 + cell
                    tallies[half * TRASH + cell] = tallies[half * TRASH + cell] + ROWS
                    return f + 1

                filled = lax.fori_loop(0, n, add, filled)
        for j in range(PAIR):
            lists[half * LIST + filled + j] = jnp.int32(TRASH)
        sizes[half] = (filled + PAIR - 1) // PAIR


def make_lists(pos, meta):
    smem = pl.BlockSpec(memory_space=pltpu.SMEM)
    return pl.pallas_call(
        lists_body,
        out_shape=[
            jax.ShapeDtypeStruct((2 * LIST + OWNERS * OWNERS,), I32),
            jax.ShapeDtypeStruct((2,), I32),
            jax.ShapeDtypeStruct((2 * TRASH,), I32),
        ],
        in_specs=[smem, smem],
        out_specs=[smem, smem, smem],
        name="lists",
    )(pos, meta)


def gram_body(half, lists, sizes, tallies, *refs):
    blocks = refs[:GROUPS]
    outs = refs[GROUPS : GROUPS + 4]
    buf, acc, acc_s, acc_q, stage, in_sems, out_sems = refs[GROUPS + 4 :]
    loads = [
        pltpu.make_async_copy(blocks[g], buf.at[pl.ds(g * SLOTS, SLOTS)], in_sems.at[g]) for g in range(GROUPS)
    ]
    for load in loads:
        load.start()

    def clear(i, _):
        acc[pl.ds(pl.multiple_of(i * ROWS, ROWS), ROWS), :] = jnp.zeros((ROWS, D), F32)
        acc_s[pl.ds(pl.multiple_of(i * 8, 8), 8), :] = jnp.zeros((8, D), F32)
        acc_q[pl.ds(pl.multiple_of(i * 8, 8), 8), :] = jnp.zeros((8, D), F32)
        return 0

    lax.fori_loop(0, TRASH + 1, clear, 0)
    for load in loads:
        load.wait()
    row = lax.broadcasted_iota(I32, (ROWS, D), 0)
    lane = lax.broadcasted_iota(I32, (ROWS, D), 1)
    upper = lane >= row

    def step(i, _):
        done = []
        for u in range(PAIR):
            entry = lists[half * LIST + i * PAIR + u]
            cell = entry & 255
            block = buf[entry >> 8]
            turned = jnp.concatenate([block[:, ROWS:], block[:, :ROWS]], axis=1)
            contract = (((0,), (0,)), ((), ()))
            top = lax.dot_general(block[:, :ROWS], block, contract, preferred_element_type=F32)
            low = lax.dot_general(block[:, ROWS:], turned, contract, preferred_element_type=F32)
            wide = block.astype(F32)
            done.append(
                (
                    cell,
                    jnp.where(upper, top, low),
                    jnp.sum(wide.reshape(8, 8, D), axis=0),
                    jnp.sum((wide * wide).reshape(8, 8, D), axis=0),
                )
            )
        for cell, gram, total, square in done:
            here = pl.ds(pl.multiple_of(cell * ROWS, ROWS), ROWS)
            acc[here, :] = acc[here, :] + gram
            near = pl.ds(pl.multiple_of(cell * 8, 8), 8)
            acc_s[near, :] = acc_s[near, :] + total
            acc_q[near, :] = acc_q[near, :] + square
        return 0

    lax.fori_loop(0, sizes[half], step, 0)
    stores = [
        pltpu.make_async_copy(acc.at[pl.ds(p * PACKED, PACKED)], outs[p].at[pl.ds(0, PACKED)], out_sems.at[p])
        for p in range(4)
    ]
    for store in stores:
        store.start()
    for p in range(4):
        base = p * 3 * CELL_DEV
        for k, source in enumerate((acc_s, acc_q)):
            total = source[pl.ds(p * CELL_DEV * 8, CELL_DEV, stride=8), :]
            for j in range(1, 8):
                total = total + source[pl.ds(p * CELL_DEV * 8 + j, CELL_DEV, stride=8), :]
            stage[pl.ds(base + k * CELL_DEV, CELL_DEV), :] = total
        for j in range(CELL_DEV):
            count = tallies[half * TRASH + p * CELL_DEV + j].astype(F32)
            stage[pl.ds(base + 2 * CELL_DEV + j, 1), :] = jnp.full((1, D), count, F32)
    tails = [
        pltpu.make_async_copy(
            stage.at[pl.ds(p * 3 * CELL_DEV, 3 * CELL_DEV)],
            outs[p].at[pl.ds(PACKED, 3 * CELL_DEV)],
            out_sems.at[4 + p],
        )
        for p in range(4)
    ]
    for tail in tails:
        tail.start()
    for copy in stores + tails:
        copy.wait()


def gram(half, lists, sizes, tallies, blocks):
    smem = pl.BlockSpec(memory_space=pltpu.SMEM)
    hbm = pl.BlockSpec(memory_space=pl.ANY)

    def body(*refs):
        gram_body(half, *refs)

    return pl.pallas_call(
        body,
        out_shape=[jax.ShapeDtypeStruct((PIECE, D), F32)] * 4,
        in_specs=[smem, smem, smem] + [hbm] * GROUPS,
        out_specs=[hbm] * 4,
        scratch_shapes=[
            pltpu.VMEM((GROUPS * SLOTS, ROWS, D), jnp.bfloat16),
            pltpu.VMEM(((TRASH + 1) * ROWS, D), F32),
            pltpu.VMEM(((TRASH + 1) * 8, D), F32),
            pltpu.VMEM(((TRASH + 1) * 8, D), F32),
            pltpu.VMEM((4 * 3 * CELL_DEV, D), F32),
            pltpu.SemaphoreType.DMA((GROUPS,)),
            pltpu.SemaphoreType.DMA((8,)),
        ],
        compiler_params=pltpu.CompilerParams(vmem_limit_bytes=VMEM_LIMIT),
        cost_estimate=pl.CostEstimate(flops=2 * 10**9, bytes_accessed=11 * 10**6, transcendentals=0),
        name=f"gram{half}",
    )(lists, sizes, tallies, *blocks)


def join_body(pos, *refs):
    parts = refs[:8]
    outs = refs[8:]
    z = pos[3]

    def total(rows):
        value = parts[0][rows, :]
        for part in parts[1:]:
            value = value + part[rows, :]
        return value

    for dz in range(NZ):
        q = lax.rem(z + dz, NZ)

        def step(i, _, dz=dz, q=q):
            outs[dz][pl.ds(pl.multiple_of(i * ROWS, ROWS), ROWS), :] = total(
                pl.ds(pl.multiple_of(q * QPACKED + i * ROWS, ROWS), ROWS)
            )
            return 0

        lax.fori_loop(0, QCELL, step, 0)
        for k in range(3):
            outs[dz][pl.ds(QPACKED + k * QCELL, QCELL), :] = total(
                pl.ds(pl.multiple_of(PACKED + k * CELL_DEV + q * QCELL, QCELL), QCELL)
            )


def join(pos, parts):
    vmem = pl.BlockSpec(memory_space=pltpu.VMEM)
    return pl.pallas_call(
        join_body,
        out_shape=[jax.ShapeDtypeStruct((QPIECE, D), F32)] * NZ,
        in_specs=[pl.BlockSpec(memory_space=pltpu.SMEM)] + [vmem] * 8,
        out_specs=[vmem] * NZ,
        compiler_params=pltpu.CompilerParams(vmem_limit_bytes=VMEM_LIMIT),
        name="join",
    )(pos, *parts)


def finish_body(pos, *refs):
    parts = refs[:NZ]
    mean_out, cov_out = refs[NZ:]
    z = pos[3]
    row = lax.broadcasted_iota(I32, (ROWS, D), 0)
    lane = lax.broadcasted_iota(I32, (ROWS, D), 1)
    for dz in range(NZ):
        q = lax.rem(z + NZ - dz, NZ)
        part = parts[dz]
        sums = part[pl.ds(QPACKED, QCELL), :]
        counts = part[pl.ds(QPACKED + 2 * QCELL, QCELL), :]
        safe = jnp.maximum(counts, 1.0)
        mean = sums / safe
        inverse = 1.0 / safe
        mean_out[pl.ds(pl.multiple_of(q * QCELL, QCELL), QCELL), :] = mean
        scaled = jnp.transpose(jnp.concatenate([mean * counts] * (D // QCELL), axis=0))
        for j in range(QCELL):
            packed = part[pl.ds(j * ROWS, ROWS), :]
            diagonal = part[pl.ds(QPACKED + QCELL + j, 1), :]
            flipped = jnp.transpose(jnp.concatenate([packed, packed], axis=0))
            rolled = pltpu.roll(packed, ROWS, 1)
            high, low = flipped[:ROWS], flipped[ROWS:]
            top = jnp.where(lane >= row, packed, high)
            corner = jnp.where(lane - ROWS < row, rolled, jnp.where(lane - ROWS == row, diagonal, high))
            bottom = jnp.where(lane < ROWS, low, corner)
            full = jnp.concatenate([top, bottom], axis=0)
            outer = scaled[:, j : j + 1] * mean[j : j + 1, :]
            cov_out[q * QCELL + j] = (full - outer) * inverse[j : j + 1, :]


def finish(pos, parts):
    vmem = pl.BlockSpec(memory_space=pltpu.VMEM)
    return pl.pallas_call(
        finish_body,
        out_shape=[
            jax.ShapeDtypeStruct((CELL_DEV, D), F32),
            jax.ShapeDtypeStruct((CELL_DEV, D, D), F32),
        ],
        in_specs=[pl.BlockSpec(memory_space=pltpu.SMEM)] + [vmem] * NZ,
        out_specs=[vmem, vmem],
        compiler_params=pltpu.CompilerParams(vmem_limit_bytes=VMEM_LIMIT),
        name="finish",
    )(pos, *parts)


def local(vectors, block_cells, dest_counts):
    x, y, c = place()
    pos = jnp.stack([x, y, c, lax.axis_index("dp")]).astype(I32)
    counts = dest_counts[0, 0]
    sent = pack(pos, counts, vectors[0])
    meta = lax.all_gather(jnp.concatenate([block_cells[0], counts]), "cell")
    halves = ([], [])
    for g, (d, dc) in enumerate(SHIFTS):
        for half in (0, 1):
            block = sent[half * GROUPS + g]
            if d or dc:
                block = lax.ppermute(block, "cell", cell_perm(d, 0, dc) if half == 0 else cell_perm(0, d, dc))
            halves[half].append(block)
    lists, sizes, tallies = make_lists(pos, meta)
    parts = []
    for half in (0, 1):
        pieces = gram(half, lists, sizes, tallies, halves[half])
        parts.append(pieces[0])
        for d in range(1, 4):
            parts.append(lax.ppermute(pieces[d], "cell", cell_perm(0, d, 0) if half == 0 else cell_perm(d, 0, 0)))
    quarters = join(pos, parts)
    mine = quarters[0]
    for dz in range(1, NZ):
        mine = mine + lax.ppermute(quarters[dz], "dp", dp_perm(dz))
    whole = [mine] + [lax.ppermute(mine, "dp", dp_perm(dz)) for dz in range(1, NZ)]
    return tuple(finish(pos, whole))


def solution(mesh):
    in_specs = (P("dp", "cell", None, None), P("dp", "cell"), P("dp", "cell", None))
    out_specs = (P("cell", None), P("cell", None, None))
    return jax.shard_map(local, mesh=mesh, in_specs=in_specs, out_specs=out_specs, check_vma=False)
```

```python
import jax
import jax.numpy as jnp
from jax import lax
from jax.experimental import pallas as pl
from jax.experimental.pallas import tpu as pltpu
from jax.sharding import PartitionSpec as P

CELLS = 1024
NX = NY = NZ = 4
NC = 2
OWNERS = NX * NY * NC
CELL_DEV = CELLS // OWNERS
BLK = 384
ROWS = 64
D = 128
RUN = 24
SLOTS = 4 * NC * RUN
SHIFTS = (0, 1, 3, 2)
GROUPS = len(SHIFTS)
CHIP_CELLS = NC * CELL_DEV
TRASH = 4 * CHIP_CELLS
SHIFT_BITS = 9
LIST = GROUPS * SLOTS + 128
PAIR = 8
F32 = jnp.float32
I32 = jnp.int32
META = 512
PACKED = CELL_DEV * ROWS
PIECE = PACKED + 3 * CELL_DEV
QCELL = CELL_DEV // NZ
QPACKED = QCELL * ROWS
QPIECE = QPACKED + 3 * QCELL
VMEM_LIMIT = 32 * 1024 * 1024

SMEM_SPEC = pl.BlockSpec(memory_space=pltpu.SMEM)
VMEM_SPEC = pl.BlockSpec(memory_space=pltpu.VMEM)
HBM_SPEC = pl.BlockSpec(memory_space=pltpu.HBM)


def at(x, y, c):
    return (x * NY + y) * NC + c


def cell_perm(even, odd, dc=0):
    steps = (even, odd)
    return [
        (at(x, y, c), at((x + steps[c][0]) % NX, (y + steps[c][1]) % NY, c ^ dc))
        for x in range(NX)
        for y in range(NY)
        for c in range(NC)
    ]


def along(d):
    return cell_perm((d, 0), (0, d))


def across(d):
    return cell_perm((0, d), (d, 0))


SWAP = cell_perm((0, 0), (0, 0), 1)


def dp_perm(dz):
    return [(z, (z + dz) % NZ) for z in range(NZ)]


def place():
    me = lax.axis_index("cell")
    x, y, c = me // (NY * NC), (me // NC) % NY, me % NC
    first, second = jnp.where(c == 0, x, y), jnp.where(c == 0, y, x)
    return jnp.stack([first, second, c, lax.axis_index("dp")]).astype(I32)


def owner(c, first, second, oc):
    return jnp.where(c == 0, at(first, second, oc), at(second, first, oc))


def pack_body(pos, counts, vectors, *refs):
    outs = refs[:GROUPS]
    offsets, sems = refs[GROUPS:]
    total = jnp.int32(0)
    for o in range(OWNERS):
        offsets[o] = total
        total = total + counts[o]
    copies = []
    for g, d in enumerate(SHIFTS):
        for k in range(4):
            for oc in range(NC):
                o = owner(pos[2], (pos[0] + d) % 4, k, oc)
                start = jnp.minimum(offsets[o], BLK - RUN)
                copies.append(
                    pltpu.make_async_copy(
                        vectors.at[pl.ds(start, RUN)],
                        outs[g].at[pl.ds((k * NC + oc) * RUN, RUN)],
                        sems.at[(g * 4 + k) * NC + oc],
                    )
                )
                copies[-1].start()
    for copy in copies:
        copy.wait()


def pack(pos, counts, vectors):
    shape = jax.ShapeDtypeStruct((SLOTS, ROWS, D), vectors.dtype)
    return pl.pallas_call(
        pack_body,
        out_shape=[shape] * GROUPS,
        in_specs=[SMEM_SPEC, SMEM_SPEC, VMEM_SPEC],
        out_specs=[HBM_SPEC] * GROUPS,
        scratch_shapes=[pltpu.SMEM((OWNERS,), I32), pltpu.SemaphoreType.DMA((OWNERS,))],
        compiler_params=pltpu.CompilerParams(vmem_limit_bytes=VMEM_LIMIT),
        name="pack",
    )(pos, counts, vectors)


def lists_body(pos, *refs):
    metas = refs[:GROUPS]
    lists, sizes, tallies, offsets = refs[GROUPS:]

    def clear(i, _):
        for u in range(8):
            tallies[i * 8 + u] = jnp.int32(0)
        return 0

    lax.fori_loop(0, TRASH // 8, clear, 0)
    for g in range(GROUPS):
        total = jnp.int32(0)
        for o in range(OWNERS):
            offsets[g * OWNERS + o] = total
            total = total + metas[g][BLK + o]
    filled = jnp.int32(0)
    begin = jnp.int32(0)
    for g in range(GROUPS):
        for k in range(4):
            for oc in range(NC):
                o = owner(pos[2], pos[0], k, oc)
                n = metas[g][BLK + o]
                start = offsets[g * OWNERS + o]
                slot = (k * NC + oc) * RUN + start - jnp.minimum(start, BLK - RUN)
                base = (lax.rem(k + 4 - pos[1], 4) * NC + lax.rem(oc + pos[2], 2)) * CELL_DEV

                def add(j, f, g=g, start=start, slot=slot, base=base):
                    cell = base + metas[g][start + j]
                    lists[f + j] = ((slot + j) << SHIFT_BITS) + cell
                    tallies[cell] = tallies[cell] + ROWS
                    return f

                lax.fori_loop(0, n, add, filled)
                filled = filled + n
        for j in range(PAIR):
            lists[filled + j] = jnp.int32(TRASH)
        sizes[2 * g] = begin
        sizes[2 * g + 1] = (filled - begin + PAIR - 1) // PAIR
        filled = begin + sizes[2 * g + 1] * PAIR
        begin = filled


def make_lists(pos, metas):
    return pl.pallas_call(
        lists_body,
        out_shape=[
            jax.ShapeDtypeStruct((LIST,), I32),
            jax.ShapeDtypeStruct((2 * GROUPS,), I32),
            jax.ShapeDtypeStruct((TRASH,), I32),
        ],
        in_specs=[SMEM_SPEC] * (1 + GROUPS),
        out_specs=[SMEM_SPEC] * 3,
        scratch_shapes=[pltpu.SMEM((GROUPS * OWNERS,), I32)],
        name="lists",
    )(pos, *metas)


def add_blocks(begin, steps, lists, buf, acc, acc_s, acc_q):
    row = lax.broadcasted_iota(I32, (ROWS, D), 0)
    lane = lax.broadcasted_iota(I32, (ROWS, D), 1)
    upper = lane >= row
    contract = (((0,), (0,)), ((), ()))

    def step(i, _):
        done = []
        for u in range(PAIR):
            entry = lists[begin + i * PAIR + u]
            cell = entry & (2**SHIFT_BITS - 1)
            block = buf[entry >> SHIFT_BITS]
            turned = jnp.concatenate([block[:, ROWS:], block[:, :ROWS]], axis=1)
            top = lax.dot_general(block[:, :ROWS], block, contract, preferred_element_type=F32)
            low = lax.dot_general(block[:, ROWS:], turned, contract, preferred_element_type=F32)
            wide = block.astype(F32)
            done.append(
                (
                    cell,
                    jnp.where(upper, top, low),
                    jnp.sum(wide.reshape(8, 8, D), axis=0),
                    jnp.sum((wide * wide).reshape(8, 8, D), axis=0),
                )
            )
        for cell, gram, total, square in done:
            here = pl.ds(pl.multiple_of(cell * ROWS, ROWS), ROWS)
            acc[here, :] = acc[here, :] + gram
            near = pl.ds(pl.multiple_of(cell * 8, 8), 8)
            acc_s[near, :] = acc_s[near, :] + total
            acc_q[near, :] = acc_q[near, :] + square
        return 0

    lax.fori_loop(0, steps, step, 0)


def early_body(lists, sizes, *refs):
    blocks = refs[: GROUPS - 1]
    acc_out, acc_s, acc_q, acc, out_sem = refs[GROUPS - 1 :]

    def clear(i, _):
        acc[pl.ds(pl.multiple_of(i * ROWS, ROWS), ROWS), :] = jnp.zeros((ROWS, D), F32)
        acc_s[pl.ds(pl.multiple_of(i * 8, 8), 8), :] = jnp.zeros((8, D), F32)
        acc_q[pl.ds(pl.multiple_of(i * 8, 8), 8), :] = jnp.zeros((8, D), F32)
        return 0

    lax.fori_loop(0, TRASH + 1, clear, 0)
    for g in range(GROUPS - 1):
        add_blocks(sizes[2 * g], sizes[2 * g + 1], lists, blocks[g], acc, acc_s, acc_q)
    store = pltpu.make_async_copy(acc, acc_out, out_sem.at[0])
    store.start()
    store.wait()


def early(lists, sizes, blocks):
    n = GROUPS - 1
    return pl.pallas_call(
        early_body,
        out_shape=[
            jax.ShapeDtypeStruct(((TRASH + 1) * ROWS, D), F32),
            jax.ShapeDtypeStruct(((TRASH + 1) * 8, D), F32),
            jax.ShapeDtypeStruct(((TRASH + 1) * 8, D), F32),
        ],
        in_specs=[SMEM_SPEC, SMEM_SPEC] + [VMEM_SPEC] * n,
        out_specs=[HBM_SPEC, VMEM_SPEC, VMEM_SPEC],
        scratch_shapes=[
            pltpu.VMEM(((TRASH + 1) * ROWS, D), F32),
            pltpu.SemaphoreType.DMA((1,)),
        ],
        compiler_params=pltpu.CompilerParams(vmem_limit_bytes=VMEM_LIMIT),
        cost_estimate=pl.CostEstimate(flops=2 * 10**9, bytes_accessed=20 * 10**6, transcendentals=0),
        name="early",
    )(lists, sizes, *blocks)


def late_body(lists, sizes, tallies, blocks, acc_in, in_s, in_q, *refs):
    outs = refs[:4]
    acc, acc_s, acc_q, stage, in_sems, out_sems = refs[4:]
    loads = [
        pltpu.make_async_copy(source, target, in_sems.at[i])
        for i, (source, target) in enumerate(((acc_in, acc), (in_s, acc_s), (in_q, acc_q)))
    ]
    for load in loads:
        load.start()
    for load in loads:
        load.wait()
    add_blocks(sizes[2 * GROUPS - 2], sizes[2 * GROUPS - 1], lists, blocks, acc, acc_s, acc_q)
    copies = []
    for part in range(4 * NC):
        copies.append(
            pltpu.make_async_copy(
                acc.at[pl.ds(part * PACKED, PACKED)],
                outs[part // NC].at[pl.ds((part % NC) * PIECE, PACKED)],
                out_sems.at[part],
            )
        )
        copies[-1].start()
    for part in range(4 * NC):
        base = part * 3 * CELL_DEV
        for k, source in enumerate((acc_s, acc_q)):
            total = source[pl.ds(part * CELL_DEV * 8, CELL_DEV, stride=8), :]
            for j in range(1, 8):
                total = total + source[pl.ds(part * CELL_DEV * 8 + j, CELL_DEV, stride=8), :]
            stage[pl.ds(base + k * CELL_DEV, CELL_DEV), :] = total
        for j in range(CELL_DEV):
            count = tallies[part * CELL_DEV + j].astype(F32)
            stage[pl.ds(base + 2 * CELL_DEV + j, 1), :] = jnp.full((1, D), count, F32)
        copies.append(
            pltpu.make_async_copy(
                stage.at[pl.ds(base, 3 * CELL_DEV)],
                outs[part // NC].at[pl.ds((part % NC) * PIECE + PACKED, 3 * CELL_DEV)],
                out_sems.at[4 * NC + part],
            )
        )
        copies[-1].start()
    for copy in copies:
        copy.wait()


def late(lists, sizes, tallies, blocks, acc, acc_s, acc_q):
    return pl.pallas_call(
        late_body,
        out_shape=[jax.ShapeDtypeStruct((NC * PIECE, D), F32)] * 4,
        in_specs=[SMEM_SPEC] * 3 + [VMEM_SPEC] + [HBM_SPEC] * 3,
        out_specs=[HBM_SPEC] * 4,
        scratch_shapes=[
            pltpu.VMEM(((TRASH + 1) * ROWS, D), F32),
            pltpu.VMEM(((TRASH + 1) * 8, D), F32),
            pltpu.VMEM(((TRASH + 1) * 8, D), F32),
            pltpu.VMEM((4 * NC * 3 * CELL_DEV, D), F32),
            pltpu.SemaphoreType.DMA((3,)),
            pltpu.SemaphoreType.DMA((8 * NC,)),
        ],
        compiler_params=pltpu.CompilerParams(vmem_limit_bytes=VMEM_LIMIT),
        cost_estimate=pl.CostEstimate(flops=10**9, bytes_accessed=20 * 10**6, transcendentals=0),
        name="late",
    )(lists, sizes, tallies, blocks, acc, acc_s, acc_q)


def total_body(*refs):
    value = refs[0][...]
    for part in refs[1:-1]:
        value = value + part[...]
    refs[-1][...] = value


def other_total(parts):
    steps = 2
    rows = PIECE // steps
    return pl.pallas_call(
        total_body,
        out_shape=jax.ShapeDtypeStruct((PIECE, D), F32),
        grid=(steps,),
        in_specs=[pl.BlockSpec((rows, D), lambda i: (steps + i, 0))] * len(parts),
        out_specs=pl.BlockSpec((rows, D), lambda i: (i, 0)),
        compiler_params=pltpu.CompilerParams(vmem_limit_bytes=VMEM_LIMIT),
        name="other_total",
    )(*parts)


def join_body(pos, *refs):
    parts = refs[:5]
    outs = refs[5:]
    z = pos[3]

    def total(rows):
        value = parts[0][rows, :]
        for part in parts[1:]:
            value = value + part[rows, :]
        return value

    for dz in range(NZ):
        q = lax.rem(z + dz, NZ)

        def step(i, _, dz=dz, q=q):
            outs[dz][pl.ds(pl.multiple_of(i * ROWS, ROWS), ROWS), :] = total(
                pl.ds(pl.multiple_of(q * QPACKED + i * ROWS, ROWS), ROWS)
            )
            return 0

        lax.fori_loop(0, QCELL, step, 0)
        for k in range(3):
            outs[dz][pl.ds(QPACKED + k * QCELL, QCELL), :] = total(
                pl.ds(pl.multiple_of(PACKED + k * CELL_DEV + q * QCELL, QCELL), QCELL)
            )


def join(pos, parts, swapped):
    own = pl.BlockSpec((PIECE, D), lambda i: (0, 0))
    quarter = pl.BlockSpec((QPIECE, D), lambda i: (0, 0))
    return pl.pallas_call(
        join_body,
        out_shape=[jax.ShapeDtypeStruct((QPIECE, D), F32)] * NZ,
        grid=(1,),
        in_specs=[SMEM_SPEC] + [own] * 5,
        out_specs=[quarter] * NZ,
        compiler_params=pltpu.CompilerParams(vmem_limit_bytes=VMEM_LIMIT),
        name="join",
    )(pos, *parts, swapped)


def finish_body(pos, *refs):
    parts = refs[:NZ]
    mean_out, cov_out = refs[NZ:]
    z = pos[3]
    row = lax.broadcasted_iota(I32, (ROWS, D), 0)
    lane = lax.broadcasted_iota(I32, (ROWS, D), 1)
    for dz in range(NZ):
        q = lax.rem(z + NZ - dz, NZ)
        part = parts[dz]
        sums = part[pl.ds(QPACKED, QCELL), :]
        counts = part[pl.ds(QPACKED + 2 * QCELL, QCELL), :]
        safe = jnp.maximum(counts, 1.0)
        mean = sums / safe
        inverse = 1.0 / safe
        mean_out[pl.ds(pl.multiple_of(q * QCELL, QCELL), QCELL), :] = mean
        scaled = jnp.transpose(jnp.concatenate([mean * counts] * (D // QCELL), axis=0))
        for j in range(QCELL):
            packed = part[pl.ds(j * ROWS, ROWS), :]
            diagonal = part[pl.ds(QPACKED + QCELL + j, 1), :]
            flipped = jnp.transpose(jnp.concatenate([packed, packed], axis=0))
            rolled = pltpu.roll(packed, ROWS, 1)
            high, low = flipped[:ROWS], flipped[ROWS:]
            top = jnp.where(lane >= row, packed, high)
            corner = jnp.where(lane - ROWS < row, rolled, jnp.where(lane - ROWS == row, diagonal, high))
            bottom = jnp.where(lane < ROWS, low, corner)
            full = jnp.concatenate([top, bottom], axis=0)
            outer = scaled[:, j : j + 1] * mean[j : j + 1, :]
            cov_out[q * QCELL + j] = (full - outer) * inverse[j : j + 1, :]


def finish(pos, parts):
    return pl.pallas_call(
        finish_body,
        out_shape=[
            jax.ShapeDtypeStruct((CELL_DEV, D), F32),
            jax.ShapeDtypeStruct((CELL_DEV, D, D), F32),
        ],
        in_specs=[SMEM_SPEC] + [VMEM_SPEC] * NZ,
        out_specs=[VMEM_SPEC, VMEM_SPEC],
        compiler_params=pltpu.CompilerParams(vmem_limit_bytes=VMEM_LIMIT),
        name="finish",
    )(pos, *parts)


def local(vectors, block_cells, dest_counts):
    pos = place()
    counts = dest_counts[0, 0]
    meta = jnp.concatenate([block_cells[0], counts, jnp.zeros((META - BLK - OWNERS,), I32)])
    metas = [meta] + [lax.ppermute(meta, "cell", along(d)) for d in SHIFTS[1:]]
    sent = pack(pos, counts, vectors[0])
    *metas, first, second = lax.optimization_barrier((*metas, sent[1], sent[2]))
    near = [sent[0], lax.ppermute(first, "cell", along(SHIFTS[1])), lax.ppermute(second, "cell", along(SHIFTS[2]))]
    held, *near = lax.optimization_barrier((sent[3], *near))
    far = lax.ppermute(held, "cell", along(SHIFTS[3]))
    lists, sizes, tallies = make_lists(pos, metas)
    pieces = late(lists, sizes, tallies, far, *early(lists, sizes, near))
    parts = [pieces[0]] + [lax.ppermute(pieces[d], "cell", across(d)) for d in range(1, 4)]
    swapped = lax.ppermute(other_total(parts), "cell", SWAP)
    quarters = join(pos, parts, swapped)
    mine = quarters[0]
    for dz in range(1, NZ):
        mine = mine + lax.ppermute(quarters[dz], "dp", dp_perm(dz))
    whole = [mine] + [lax.ppermute(mine, "dp", dp_perm(dz)) for dz in range(1, NZ)]
    return tuple(finish(pos, whole))


def solution(mesh):
    in_specs = (P("dp", "cell", None, None), P("dp", "cell"), P("dp", "cell", None))
    out_specs = (P("cell", None), P("cell", None, None))
    return jax.shard_map(local, mesh=mesh, in_specs=in_specs, out_specs=out_specs, check_vma=False)
```

```python
import jax
import jax.numpy as jnp
from jax import lax
from jax.experimental import pallas as pl
from jax.experimental.pallas import tpu as pltpu
from jax.sharding import PartitionSpec as P

CELLS = 1024
NX = NY = NZ = 4
NC = 2
OWNERS = NX * NY * NC
CELL_DEV = CELLS // OWNERS
BLK = 384
ROWS = 64
D = 128
RUN = 24
SLOTS = NC * RUN
SHIFTS = (0, 1, 3, 2)
GROUPS = len(SHIFTS)
CHIP_CELLS = NC * CELL_DEV
LIST = 4 * GROUPS * SLOTS + 128
PAIR = 8
F32 = jnp.float32
I32 = jnp.int32
META = 512
UNITS = (((2, 0), (2, 1)), ((0, 0), (0, 1)), ((1, 1), (3, 0)), ((1, 0), (3, 1)))
PACKED = CELL_DEV * ROWS
PIECE = PACKED + 3 * CELL_DEV
QCELL = CELL_DEV // NZ
QPACKED = QCELL * ROWS
QPIECE = QPACKED + 3 * QCELL
VMEM_LIMIT = 16 * 1024 * 1024
LARGE_VMEM = 56 * 1024 * 1024
SMALL_VMEM = 6 * 1024 * 1024

SMEM_SPEC = pl.BlockSpec(memory_space=pltpu.SMEM)
VMEM_SPEC = pl.BlockSpec(memory_space=pltpu.VMEM)
HBM_SPEC = pl.BlockSpec(memory_space=pltpu.HBM)


def at(x, y, c):
    return (x * NY + y) * NC + c


def cell_perm(even, odd, dc=0):
    steps = (even, odd)
    return [
        (at(x, y, c), at((x + steps[c][0]) % NX, (y + steps[c][1]) % NY, c ^ dc))
        for x in range(NX)
        for y in range(NY)
        for c in range(NC)
    ]


def along(d):
    return cell_perm((d, 0), (0, d))


def across(d):
    return cell_perm((0, d), (d, 0))


SWAP = cell_perm((0, 0), (0, 0), 1)


def dp_perm(dz):
    return [(z, (z + dz) % NZ) for z in range(NZ)]


def place():
    me = lax.axis_index("cell")
    x, y, c = me // (NY * NC), (me // NC) % NY, me % NC
    first, second = jnp.where(c == 0, x, y), jnp.where(c == 0, y, x)
    return jnp.stack([first, second, c, lax.axis_index("dp")]).astype(I32)


def owner(c, first, second, oc):
    return jnp.where(c == 0, at(first, second, oc), at(second, first, oc))


def unit_owner(pos, d, rel, side):
    return owner(pos[2], lax.rem(pos[0] + d, 4), lax.rem(pos[1] + rel, 4), lax.rem(pos[2] + side, 2))


def gather_body(flows, pos, counts, vectors, *refs):
    outs = refs[: len(flows)]
    offsets, sems = refs[len(flows) :]
    total = jnp.int32(0)
    for o in range(OWNERS):
        offsets[o] = total
        total = total + counts[o]
    copies = []
    for out, (d, units) in zip(outs, flows):
        for i, (rel, side) in enumerate(units):
            o = unit_owner(pos, d, rel, side)
            start = jnp.minimum(offsets[o], BLK - RUN)
            copies.append(
                pltpu.make_async_copy(vectors.at[pl.ds(start, RUN)], out.at[pl.ds(i * RUN, RUN)], sems.at[len(copies)])
            )
            copies[-1].start()
    for copy in copies:
        copy.wait()


def gather_runs(flows, pos, counts, vectors, name, vmem):
    def body(*refs):
        gather_body(flows, *refs)

    return pl.pallas_call(
        body,
        out_shape=[jax.ShapeDtypeStruct((SLOTS, ROWS, D), vectors.dtype)] * len(flows),
        in_specs=[SMEM_SPEC, SMEM_SPEC, HBM_SPEC],
        out_specs=[VMEM_SPEC] * len(flows),
        scratch_shapes=[pltpu.SMEM((OWNERS,), I32), pltpu.SemaphoreType.DMA((NC * len(flows),))],
        compiler_params=pltpu.CompilerParams(vmem_limit_bytes=vmem),
        name=name,
    )(pos, counts, vectors)


def lists_body(pos, *refs):
    metas = refs[:GROUPS]
    lists, sizes, tallies, offsets = refs[GROUPS:]

    def clear(i, _):
        for u in range(8):
            tallies[i * 8 + u] = jnp.int32(0)
        return 0

    lax.fori_loop(0, 4 * CHIP_CELLS // 8, clear, 0)
    for g in range(GROUPS):
        total = jnp.int32(0)
        for o in range(OWNERS):
            offsets[g * OWNERS + o] = total
            total = total + metas[g][BLK + o]
    begin = jnp.int32(0)
    for group, units in enumerate(UNITS):
        for g in range(GROUPS):
            filled = begin
            for i, (rel, side) in enumerate(units):
                o = unit_owner(pos, 0, rel, side)
                n = metas[g][BLK + o]
                start = offsets[g * OWNERS + o]
                slot = i * RUN + start - jnp.minimum(start, BLK - RUN)
                base = (slot << 17) + i * ((PIECE // 8 << 7) + CELL_DEV)
                tally = group * CHIP_CELLS + i * CELL_DEV

                def add(j, f, g=g, start=start, base=base, tally=tally):
                    cell = metas[g][start + j]
                    lists[f + j] = base + (j << 17) + cell * ((ROWS // 8 << 7) + 1)
                    tallies[tally + cell] = tallies[tally + cell] + ROWS
                    return f

                lax.fori_loop(0, n, add, filled)
                filled = filled + n
            for j in range(PAIR):
                lists[filled + j] = jnp.int32((PACKED // 8 << 7) + CHIP_CELLS)
            segment = group * GROUPS + g
            sizes[2 * segment] = begin
            sizes[2 * segment + 1] = (filled - begin + PAIR - 1) // PAIR
            begin = begin + sizes[2 * segment + 1] * PAIR


def make_lists(pos, metas):
    return pl.pallas_call(
        lists_body,
        out_shape=[
            jax.ShapeDtypeStruct((LIST,), I32),
            jax.ShapeDtypeStruct((8 * GROUPS,), I32),
            jax.ShapeDtypeStruct((4 * CHIP_CELLS,), I32),
        ],
        in_specs=[SMEM_SPEC] * (1 + GROUPS),
        out_specs=[SMEM_SPEC] * 3,
        scratch_shapes=[pltpu.SMEM((GROUPS * OWNERS,), I32)],
        compiler_params=pltpu.CompilerParams(vmem_limit_bytes=SMALL_VMEM),
        name="lists",
    )(pos, *metas)


def add_blocks(segment, lists, sizes, buf, acc, acc_s, acc_q):
    begin, steps = sizes[2 * segment], sizes[2 * segment + 1]
    row = lax.broadcasted_iota(I32, (ROWS, D), 0)
    lane = lax.broadcasted_iota(I32, (ROWS, D), 1)
    upper = lane >= row
    contract = (((0,), (0,)), ((), ()))

    def step(i, _):
        done = []
        for u in range(PAIR):
            entry = lists[begin + i * PAIR + u]
            block = buf[entry >> 17]
            turned = jnp.concatenate([block[:, ROWS:], block[:, :ROWS]], axis=1)
            top = lax.dot_general(block[:, :ROWS], block, contract, preferred_element_type=F32)
            low = lax.dot_general(block[:, ROWS:], turned, contract, preferred_element_type=F32)
            wide = block.astype(F32)
            done.append(
                (
                    pl.multiple_of(((entry >> 7) & 1023) * 8, 8),
                    pl.multiple_of((entry & 127) * 8, 8),
                    jnp.where(upper, top, low),
                    jnp.sum(wide.reshape(8, 8, D), axis=0),
                    jnp.sum((wide * wide).reshape(8, 8, D), axis=0),
                )
            )
        for at_row, at_sum, gram, total, square in done:
            here, near = pl.ds(at_row, ROWS), pl.ds(at_sum, 8)
            acc[here, :] = acc[here, :] + gram
            acc_s[near, :] = acc_s[near, :] + total
            acc_q[near, :] = acc_q[near, :] + square
        return 0

    lax.fori_loop(0, steps, step, 0)


def gram_body(group, started, lists, sizes, tallies, *refs):
    blocks = refs[:GROUPS]
    starts = refs[GROUPS : GROUPS + started]
    outs = refs[GROUPS + started : GROUPS + started + 2]
    acc, acc_s, acc_q = refs[GROUPS + started + 2 :]

    def clear(i, _):
        rows = pl.ds(pl.multiple_of(i * ROWS, ROWS), ROWS)
        for u in range(2):
            value = starts[u][rows, :] if started else jnp.zeros((ROWS, D), F32)
            acc[pl.ds(pl.multiple_of(u * PIECE + i * ROWS, 8), ROWS), :] = value
        return 0

    lax.fori_loop(0, CELL_DEV, clear, 0)

    def clear_sums(i, _):
        acc_s[pl.ds(pl.multiple_of(i * 8, 8), 8), :] = jnp.zeros((8, D), F32)
        acc_q[pl.ds(pl.multiple_of(i * 8, 8), 8), :] = jnp.zeros((8, D), F32)
        return 0

    lax.fori_loop(0, CHIP_CELLS, clear_sums, 0)
    for g in range(GROUPS):
        add_blocks(group * GROUPS + g, lists, sizes, blocks[g], acc, acc_s, acc_q)

    def copy_out(i, _):
        rows = pl.ds(pl.multiple_of(i * ROWS, ROWS), ROWS)
        for u in range(2):
            outs[u][rows, :] = acc[pl.ds(pl.multiple_of(u * PIECE + i * ROWS, 8), ROWS), :]
        return 0

    lax.fori_loop(0, CELL_DEV, copy_out, 0)
    for u in range(2):
        for k, source in enumerate((acc_s, acc_q)):
            total = source[pl.ds(u * CELL_DEV * 8, CELL_DEV, stride=8), :]
            for j in range(1, 8):
                total = total + source[pl.ds(u * CELL_DEV * 8 + j, CELL_DEV, stride=8), :]
            rows = pl.ds(PACKED + k * CELL_DEV, CELL_DEV)
            outs[u][rows, :] = total + starts[u][rows, :] if started else total
        for j in range(CELL_DEV):
            count = jnp.full((1, D), tallies[group * CHIP_CELLS + u * CELL_DEV + j].astype(F32), F32)
            rows = pl.ds(PACKED + 2 * CELL_DEV + j, 1)
            outs[u][rows, :] = count + starts[u][rows, :] if started else count


def gram(group, lists, sizes, tallies, blocks, starts=()):
    def body(*refs):
        gram_body(group, len(starts), *refs)

    half = jax.ShapeDtypeStruct((PIECE, D), F32)
    return pl.pallas_call(
        body,
        out_shape=[half, half],
        in_specs=[SMEM_SPEC] * 3 + [VMEM_SPEC] * (GROUPS + len(starts)),
        out_specs=[VMEM_SPEC] * 2,
        scratch_shapes=[pltpu.VMEM((NC * PIECE, D), F32)] + [pltpu.VMEM(((CHIP_CELLS + 1) * 8, D), F32)] * 2,
        compiler_params=pltpu.CompilerParams(vmem_limit_bytes=SMALL_VMEM),
        cost_estimate=pl.CostEstimate(flops=10**9, bytes_accessed=10**7, transcendentals=0),
        name=f"gram{group}",
    )(lists, sizes, tallies, *blocks, *starts)


def total_body(*refs):
    def step(i, _):
        rows = pl.ds(pl.multiple_of(i * 32, 32), 32)
        value = refs[0][rows, :]
        for part in refs[1:-1]:
            value = value + part[rows, :]
        refs[-1][rows, :] = value
        return 0

    lax.fori_loop(0, PIECE // 32, step, 0)


def other_total(parts):
    return pl.pallas_call(
        total_body,
        out_shape=jax.ShapeDtypeStruct((PIECE, D), F32),
        in_specs=[VMEM_SPEC] * len(parts),
        out_specs=VMEM_SPEC,
        compiler_params=pltpu.CompilerParams(vmem_limit_bytes=SMALL_VMEM),
        name="other_total",
    )(*parts)


def join_body(pos, *refs):
    outs = refs[-NZ:]
    parts = refs[:-NZ]
    z = pos[3]

    def total(rows):
        value = parts[0][rows, :]
        for part in parts[1:]:
            value = value + part[rows, :]
        return value

    for dz in range(NZ):
        q = lax.rem(z + dz, NZ)

        def step(i, _, dz=dz, q=q):
            outs[dz][pl.ds(pl.multiple_of(i * ROWS, ROWS), ROWS), :] = total(
                pl.ds(pl.multiple_of(q * QPACKED + i * ROWS, ROWS), ROWS)
            )
            return 0

        lax.fori_loop(0, QCELL, step, 0)
        for k in range(3):
            outs[dz][pl.ds(QPACKED + k * QCELL, QCELL), :] = total(
                pl.ds(pl.multiple_of(PACKED + k * CELL_DEV + q * QCELL, QCELL), QCELL)
            )


def join(pos, parts):
    return pl.pallas_call(
        join_body,
        out_shape=[jax.ShapeDtypeStruct((QPIECE, D), F32)] * NZ,
        in_specs=[SMEM_SPEC] + [VMEM_SPEC] * len(parts),
        out_specs=[VMEM_SPEC] * NZ,
        compiler_params=pltpu.CompilerParams(vmem_limit_bytes=SMALL_VMEM),
        name="join",
    )(pos, *parts)


def finish_body(pos, *refs):
    parts = refs[:NZ]
    mean_out, cov_out = refs[NZ:]
    z = pos[3]
    row = lax.broadcasted_iota(I32, (ROWS, D), 0)
    lane = lax.broadcasted_iota(I32, (ROWS, D), 1)
    for dz in range(NZ):
        q = lax.rem(z + NZ - dz, NZ)
        part = parts[dz]
        sums = part[pl.ds(QPACKED, QCELL), :]
        counts = part[pl.ds(QPACKED + 2 * QCELL, QCELL), :]
        safe = jnp.maximum(counts, 1.0)
        mean = sums / safe
        inverse = 1.0 / safe
        mean_out[pl.ds(pl.multiple_of(q * QCELL, QCELL), QCELL), :] = mean
        scaled = jnp.transpose(jnp.concatenate([mean * counts] * (D // QCELL), axis=0))
        for j in range(QCELL):
            packed = part[pl.ds(j * ROWS, ROWS), :]
            diagonal = part[pl.ds(QPACKED + QCELL + j, 1), :]
            flipped = jnp.transpose(jnp.concatenate([packed, packed], axis=0))
            rolled = pltpu.roll(packed, ROWS, 1)
            high, low = flipped[:ROWS], flipped[ROWS:]
            top = jnp.where(lane >= row, packed, high)
            corner = jnp.where(lane - ROWS < row, rolled, jnp.where(lane - ROWS == row, diagonal, high))
            bottom = jnp.where(lane < ROWS, low, corner)
            full = jnp.concatenate([top, bottom], axis=0)
            outer = scaled[:, j : j + 1] * mean[j : j + 1, :]
            cov_out[q * QCELL + j] = (full - outer) * inverse[j : j + 1, :]


def finish(pos, parts):
    return pl.pallas_call(
        finish_body,
        out_shape=[
            jax.ShapeDtypeStruct((CELL_DEV, D), F32),
            jax.ShapeDtypeStruct((CELL_DEV, D, D), F32),
        ],
        in_specs=[SMEM_SPEC] + [VMEM_SPEC] * NZ,
        out_specs=[VMEM_SPEC, VMEM_SPEC],
        compiler_params=pltpu.CompilerParams(vmem_limit_bytes=VMEM_LIMIT),
        name="finish",
    )(pos, *parts)


def local(vectors, block_cells, dest_counts):
    pos = place()
    counts = dest_counts[0, 0]
    meta = jnp.concatenate([block_cells[0], counts, jnp.zeros((META - BLK - OWNERS,), I32)])
    metas = [meta] + [lax.ppermute(meta, "cell", along(d)) for d in SHIFTS[1:]]
    lists, sizes, tallies = make_lists(pos, metas)
    sent, got = [], []
    for group, units in enumerate(UNITS):
        turn = pos
        if group == 1:
            turn, *_ = lax.optimization_barrier((pos, *sent[0]))
        elif group > 1:
            turn, *_ = lax.optimization_barrier((pos, sizes, *got[group - 2][1:]))
        runs = gather_runs([(d, units) for d in SHIFTS], turn, counts, vectors[0], f"gather{group}", LARGE_VMEM if group == 0 else SMALL_VMEM)
        if group == 0:
            *_, r0, r1, r2, r3 = lax.optimization_barrier((*metas, *runs))
            runs = [r0, r1, r2, r3]
        sent.append(runs)
        got.append([runs[0]] + [lax.ppermute(run, "cell", along(d)) for d, run in zip(SHIFTS[1:], runs[1:])])

    def step(rel, piece):
        return lax.ppermute(piece, "cell", across(rel))

    fore, back = gram(0, lists, sizes, tallies, got[0])
    fore, back = step(1, fore), step(3, back)
    left, right = gram(2, lists, sizes, tallies, got[2])
    other1, own3 = step(1, left), step(3, right)
    left, right = gram(3, lists, sizes, tallies, got[3], (fore, back))
    own1, other3 = step(1, left), step(3, right)
    own, other = gram(1, lists, sizes, tallies, got[1], (own3, other1))
    swapped = lax.ppermute(other_total([other, other3]), "cell", SWAP)
    quarters = join(pos, [own, own1, swapped])
    mine = quarters[0]
    for dz in range(1, NZ):
        mine = mine + lax.ppermute(quarters[dz], "dp", dp_perm(dz))
    whole = [mine] + [lax.ppermute(mine, "dp", dp_perm(dz)) for dz in range(1, NZ)]
    return tuple(finish(pos, whole))


def solution(mesh):
    in_specs = (P("dp", "cell", None, None), P("dp", "cell"), P("dp", "cell", None))
    out_specs = (P("cell", None), P("cell", None, None))
    return jax.shard_map(local, mesh=mesh, in_specs=in_specs, out_specs=out_specs, check_vma=False)
```

```python
import jax
import jax.numpy as jnp
from jax import lax
from jax.experimental import pallas as pl
from jax.experimental.pallas import tpu as pltpu
from jax.sharding import PartitionSpec as P

CELLS = 1024
NX = NY = NZ = 4
NC = 2
OWNERS = NX * NY * NC
CELL_DEV = CELLS // OWNERS
BLK = 384
ROWS = 64
D = 128
RUN = 24
SLOTS = NC * RUN
SHIFTS = (0, 1, 3, 2)
COPIES = 1
GROUPS = len(SHIFTS)
CHIP_CELLS = NC * CELL_DEV
LIST = 4 * GROUPS * SLOTS + 128
PAIR = 8
F32 = jnp.float32
I32 = jnp.int32
HEAD = 16
UNITS = (((2, 0), (2, 1)), ((0, 0), (0, 1)), ((1, 1), (3, 0)), ((1, 0), (3, 1)))
PACKED = CELL_DEV * ROWS
PIECE = PACKED + 3 * CELL_DEV
QCELL = CELL_DEV // NZ
QPACKED = QCELL * ROWS
QPIECE = QPACKED + 3 * QCELL
VMEM_LIMIT = 16 * 1024 * 1024
LARGE_VMEM = 56 * 1024 * 1024
SMALL_VMEM = 6 * 1024 * 1024

SMEM_SPEC = pl.BlockSpec(memory_space=pltpu.SMEM)
VMEM_SPEC = pl.BlockSpec(memory_space=pltpu.VMEM)
HBM_SPEC = pl.BlockSpec(memory_space=pltpu.HBM)


def at(x, y, c):
    return (x * NY + y) * NC + c


def cell_perm(even, odd, dc=0):
    steps = (even, odd)
    return [
        (at(x, y, c), at((x + steps[c][0]) % NX, (y + steps[c][1]) % NY, c ^ dc))
        for x in range(NX)
        for y in range(NY)
        for c in range(NC)
    ]


def along(d):
    return cell_perm((d, 0), (0, d))


def across(d):
    return cell_perm((0, d), (d, 0))


SWAP = cell_perm((0, 0), (0, 0), 1)


def dp_perm(dz):
    return [(z, (z + dz) % NZ) for z in range(NZ)]


def place():
    me = lax.axis_index("cell")
    x, y, c = me // (NY * NC), (me // NC) % NY, me % NC
    first, second = jnp.where(c == 0, x, y), jnp.where(c == 0, y, x)
    return jnp.stack([first, second, c, lax.axis_index("dp")]).astype(I32)


def owner(c, first, second, oc):
    return jnp.where(c == 0, at(first, second, oc), at(second, first, oc))


def unit_owner(pos, d, rel, side):
    return owner(pos[2], lax.rem(pos[0] + d, 4), lax.rem(pos[1] + rel, 4), lax.rem(pos[2] + side, 2))


def gather_body(flows, head, pos, counts, vectors, *refs):
    header, refs = (refs[:2], refs[2:]) if head else ((), refs)
    outs = refs[: len(flows)]
    offsets, sems = refs[len(flows) : len(flows) + 2]
    total = jnp.int32(0)
    for o in range(OWNERS):
        offsets[o] = total
        total = total + counts[o]
    copies = []
    rows = RUN * ROWS // COPIES
    for out, (d, units) in zip(outs, flows):
        for i, (rel, side) in enumerate(units):
            start = jnp.minimum(offsets[unit_owner(pos, d, rel, side)], BLK - RUN)
            for part in range(COPIES):
                copies.append(
                    pltpu.make_async_copy(
                        vectors.at[pl.ds(pl.multiple_of(start * ROWS + part * rows, ROWS), rows)],
                        out.at[pl.ds((i * COPIES + part) * rows, rows)],
                        sems.at[len(copies)],
                    )
                )
                copies[-1].start()
    if head:
        cells, count_row = header
        text = refs[-1]
        text[...] = jnp.zeros((HEAD, D), F32)
        for i in range(BLK // D):
            text[i : i + 1, :] = cells[:, i * D : (i + 1) * D].astype(F32)
        text[BLK // D : BLK // D + 1, :OWNERS] = count_row[...].astype(F32)
        for out in outs:
            out[pl.ds(SLOTS * ROWS, HEAD), :] = text[...].astype(out.dtype)
    for copy in copies:
        copy.wait()


def gather_runs(flows, pos, counts, vectors, name, header=()):
    def body(*refs):
        gather_body(flows, bool(header), *refs)

    rows = SLOTS * ROWS + (HEAD if header else 0)
    return pl.pallas_call(
        body,
        out_shape=[jax.ShapeDtypeStruct((rows, D), vectors.dtype)] * len(flows),
        in_specs=[SMEM_SPEC, SMEM_SPEC, HBM_SPEC] + [VMEM_SPEC] * len(header),
        out_specs=[VMEM_SPEC] * len(flows),
        scratch_shapes=[pltpu.SMEM((OWNERS,), I32), pltpu.SemaphoreType.DMA((2 * COPIES * len(flows),))]
        + ([pltpu.VMEM((HEAD, D), F32)] if header else []),
        compiler_params=pltpu.CompilerParams(vmem_limit_bytes=LARGE_VMEM if header else SMALL_VMEM),
        name=name,
    )(pos, counts, vectors, *header)


def lists_body(pos, own_cells, own_counts, *refs):
    heads = refs[: GROUPS - 1]
    lists, sizes, tallies, offsets, text, metas, sem = refs[GROUPS - 1 :]
    for g, head in enumerate(heads):
        text[pl.ds(g * 8, 8), :] = head[...].astype(F32)[:8].astype(I32)
    copy = pltpu.make_async_copy(text, metas, sem.at[0])
    copy.start()

    def clear(i, _):
        for u in range(8):
            tallies[i * 8 + u] = jnp.int32(0)
        return 0

    lax.fori_loop(0, 4 * CHIP_CELLS // 8, clear, 0)
    copy.wait()

    def count_of(g, o):
        return own_counts[o] if g == 0 else metas[(g - 1) * 8 + BLK // D, o]

    def cell_of(g, i):
        return own_cells[i] if g == 0 else metas[(g - 1) * 8 + (i >> 7), i & (D - 1)]

    for g in range(GROUPS):
        total = jnp.int32(0)
        for o in range(OWNERS):
            offsets[g * OWNERS + o] = total
            total = total + count_of(g, o)
    begin = jnp.int32(0)
    for group, units in enumerate(UNITS):
        for g in range(GROUPS):
            filled = begin
            for i, (rel, side) in enumerate(units):
                o = unit_owner(pos, 0, rel, side)
                n = count_of(g, o)
                start = offsets[g * OWNERS + o]
                slot = i * RUN + start - jnp.minimum(start, BLK - RUN)
                base = (slot << 17) + i * ((PIECE // 8 << 7) + CELL_DEV)
                tally = group * CHIP_CELLS + i * CELL_DEV

                def add(j, f, g=g, start=start, base=base, tally=tally):
                    cell = cell_of(g, start + j)
                    lists[f + j] = base + (j << 17) + cell * ((ROWS // 8 << 7) + 1)
                    tallies[tally + cell] = tallies[tally + cell] + ROWS
                    return f

                lax.fori_loop(0, n, add, filled)
                filled = filled + n
            for j in range(PAIR):
                lists[filled + j] = jnp.int32((PACKED // 8 << 7) + CHIP_CELLS)
            segment = group * GROUPS + g
            sizes[2 * segment] = begin
            sizes[2 * segment + 1] = (filled - begin + PAIR - 1) // PAIR
            begin = begin + sizes[2 * segment + 1] * PAIR


def make_lists(pos, own_cells, own_counts, arrived):
    head = pl.BlockSpec((HEAD, D), lambda i: (SLOTS * ROWS // HEAD, 0))
    return pl.pallas_call(
        lists_body,
        out_shape=[
            jax.ShapeDtypeStruct((LIST,), I32),
            jax.ShapeDtypeStruct((8 * GROUPS,), I32),
            jax.ShapeDtypeStruct((4 * CHIP_CELLS,), I32),
        ],
        grid=(1,),
        in_specs=[SMEM_SPEC] * 3 + [head] * (GROUPS - 1),
        out_specs=[SMEM_SPEC] * 3,
        scratch_shapes=[
            pltpu.SMEM((GROUPS * OWNERS,), I32),
            pltpu.VMEM(((GROUPS - 1) * 8, D), I32),
            pltpu.SMEM(((GROUPS - 1) * 8, D), I32),
            pltpu.SemaphoreType.DMA((1,)),
        ],
        compiler_params=pltpu.CompilerParams(vmem_limit_bytes=SMALL_VMEM),
        name="lists",
    )(pos, own_cells, own_counts, *arrived)


def add_blocks(segment, lists, sizes, buf, acc, acc_s, acc_q):
    begin, steps = sizes[2 * segment], sizes[2 * segment + 1]
    row = lax.broadcasted_iota(I32, (ROWS, D), 0)
    lane = lax.broadcasted_iota(I32, (ROWS, D), 1)
    upper = lane >= row
    contract = (((0,), (0,)), ((), ()))

    def step(i, _):
        done = []
        for u in range(PAIR):
            entry = lists[begin + i * PAIR + u]
            block = buf[pl.ds(pl.multiple_of((entry >> 17) * ROWS, ROWS), ROWS), :]
            turned = jnp.concatenate([block[:, ROWS:], block[:, :ROWS]], axis=1)
            top = lax.dot_general(block[:, :ROWS], block, contract, preferred_element_type=F32)
            low = lax.dot_general(block[:, ROWS:], turned, contract, preferred_element_type=F32)
            wide = block.astype(F32)
            done.append(
                (
                    pl.multiple_of(((entry >> 7) & 1023) * 8, 8),
                    pl.multiple_of((entry & 127) * 8, 8),
                    jnp.where(upper, top, low),
                    jnp.sum(wide.reshape(8, 8, D), axis=0),
                    jnp.sum((wide * wide).reshape(8, 8, D), axis=0),
                )
            )
        for at_row, at_sum, gram, total, square in done:
            here, near = pl.ds(at_row, ROWS), pl.ds(at_sum, 8)
            acc[here, :] = acc[here, :] + gram
            acc_s[near, :] = acc_s[near, :] + total
            acc_q[near, :] = acc_q[near, :] + square
        return 0

    lax.fori_loop(0, steps, step, 0)


def gram_body(group, started, lists, sizes, tallies, *refs):
    blocks = refs[:GROUPS]
    first, second = started
    starts = (refs[GROUPS : GROUPS + first], refs[GROUPS + first : GROUPS + first + second])
    outs = refs[GROUPS + first + second :][:2]
    acc, acc_s, acc_q = refs[GROUPS + first + second + 2 :]

    def add_starts(value, u, rows):
        for start in starts[u]:
            value = value + start[rows, :]
        return value

    def clear(i, _):
        rows = pl.ds(pl.multiple_of(i * ROWS, ROWS), ROWS)
        for u in range(2):
            value = add_starts(jnp.zeros((ROWS, D), F32), u, rows)
            acc[pl.ds(pl.multiple_of(u * PIECE + i * ROWS, 8), ROWS), :] = value
        return 0

    lax.fori_loop(0, CELL_DEV, clear, 0)

    def clear_sums(i, _):
        acc_s[pl.ds(pl.multiple_of(i * 8, 8), 8), :] = jnp.zeros((8, D), F32)
        acc_q[pl.ds(pl.multiple_of(i * 8, 8), 8), :] = jnp.zeros((8, D), F32)
        return 0

    lax.fori_loop(0, CHIP_CELLS, clear_sums, 0)
    for g in range(GROUPS):
        add_blocks(group * GROUPS + g, lists, sizes, blocks[g], acc, acc_s, acc_q)

    def copy_out(i, _):
        rows = pl.ds(pl.multiple_of(i * ROWS, ROWS), ROWS)
        for u in range(2):
            outs[u][rows, :] = acc[pl.ds(pl.multiple_of(u * PIECE + i * ROWS, 8), ROWS), :]
        return 0

    lax.fori_loop(0, CELL_DEV, copy_out, 0)
    for u in range(2):
        for k, source in enumerate((acc_s, acc_q)):
            total = source[pl.ds(u * CELL_DEV * 8, CELL_DEV, stride=8), :]
            for j in range(1, 8):
                total = total + source[pl.ds(u * CELL_DEV * 8 + j, CELL_DEV, stride=8), :]
            rows = pl.ds(PACKED + k * CELL_DEV, CELL_DEV)
            outs[u][rows, :] = add_starts(total, u, rows)
        for j in range(CELL_DEV):
            count = jnp.full((1, D), tallies[group * CHIP_CELLS + u * CELL_DEV + j].astype(F32), F32)
            rows = pl.ds(PACKED + 2 * CELL_DEV + j, 1)
            outs[u][rows, :] = add_starts(count, u, rows)


def gram(group, lists, sizes, tallies, blocks, first=(), second=()):
    def body(*refs):
        gram_body(group, (len(first), len(second)), *refs)

    half = jax.ShapeDtypeStruct((PIECE, D), F32)
    return pl.pallas_call(
        body,
        out_shape=[half, half],
        in_specs=[SMEM_SPEC] * 3 + [VMEM_SPEC] * (GROUPS + len(first) + len(second)),
        out_specs=[VMEM_SPEC] * 2,
        scratch_shapes=[pltpu.VMEM((NC * PIECE, D), F32)] + [pltpu.VMEM(((CHIP_CELLS + 1) * 8, D), F32)] * 2,
        compiler_params=pltpu.CompilerParams(vmem_limit_bytes=SMALL_VMEM),
        cost_estimate=pl.CostEstimate(flops=10**9, bytes_accessed=10**7, transcendentals=0),
        name=f"gram{group}",
    )(lists, sizes, tallies, *blocks, *first, *second)


def total_body(*refs):
    def step(i, _):
        rows = pl.ds(pl.multiple_of(i * 32, 32), 32)
        value = refs[0][rows, :]
        for part in refs[1:-1]:
            value = value + part[rows, :]
        refs[-1][rows, :] = value
        return 0

    lax.fori_loop(0, PIECE // 32, step, 0)


def other_total(parts):
    return pl.pallas_call(
        total_body,
        out_shape=jax.ShapeDtypeStruct((PIECE, D), F32),
        in_specs=[VMEM_SPEC] * len(parts),
        out_specs=VMEM_SPEC,
        compiler_params=pltpu.CompilerParams(vmem_limit_bytes=SMALL_VMEM),
        name="other_total",
    )(*parts)


def join_body(pos, *refs):
    outs = refs[-NZ:]
    parts = refs[:-NZ]
    z = pos[3]

    def total(rows):
        value = parts[0][rows, :]
        for part in parts[1:]:
            value = value + part[rows, :]
        return value

    for dz in range(NZ):
        q = lax.rem(z + dz, NZ)

        def step(i, _, dz=dz, q=q):
            outs[dz][pl.ds(pl.multiple_of(i * ROWS, ROWS), ROWS), :] = total(
                pl.ds(pl.multiple_of(q * QPACKED + i * ROWS, ROWS), ROWS)
            )
            return 0

        lax.fori_loop(0, QCELL, step, 0)
        for k in range(3):
            outs[dz][pl.ds(QPACKED + k * QCELL, QCELL), :] = total(
                pl.ds(pl.multiple_of(PACKED + k * CELL_DEV + q * QCELL, QCELL), QCELL)
            )


def join(pos, parts):
    return pl.pallas_call(
        join_body,
        out_shape=[jax.ShapeDtypeStruct((QPIECE, D), F32)] * NZ,
        in_specs=[SMEM_SPEC] + [VMEM_SPEC] * len(parts),
        out_specs=[VMEM_SPEC] * NZ,
        compiler_params=pltpu.CompilerParams(vmem_limit_bytes=SMALL_VMEM),
        name="join",
    )(pos, *parts)


def finish_body(pos, *refs):
    parts = refs[:NZ]
    mean_out, cov_out = refs[NZ:]
    z = pos[3]
    row = lax.broadcasted_iota(I32, (ROWS, D), 0)
    lane = lax.broadcasted_iota(I32, (ROWS, D), 1)
    for dz in range(NZ):
        q = lax.rem(z + NZ - dz, NZ)
        part = parts[dz]
        sums = part[pl.ds(QPACKED, QCELL), :]
        counts = part[pl.ds(QPACKED + 2 * QCELL, QCELL), :]
        safe = jnp.maximum(counts, 1.0)
        mean = sums / safe
        inverse = 1.0 / safe
        mean_out[pl.ds(pl.multiple_of(q * QCELL, QCELL), QCELL), :] = mean
        scaled = jnp.transpose(jnp.concatenate([mean * counts] * (D // QCELL), axis=0))
        for j in range(QCELL):
            packed = part[pl.ds(j * ROWS, ROWS), :]
            diagonal = part[pl.ds(QPACKED + QCELL + j, 1), :]
            flipped = jnp.transpose(jnp.concatenate([packed, packed], axis=0))
            rolled = pltpu.roll(packed, ROWS, 1)
            high, low = flipped[:ROWS], flipped[ROWS:]
            top = jnp.where(lane >= row, packed, high)
            corner = jnp.where(lane - ROWS < row, rolled, jnp.where(lane - ROWS == row, diagonal, high))
            bottom = jnp.where(lane < ROWS, low, corner)
            full = jnp.concatenate([top, bottom], axis=0)
            outer = scaled[:, j : j + 1] * mean[j : j + 1, :]
            cov_out[q * QCELL + j] = (full - outer) * inverse[j : j + 1, :]


def finish(pos, parts):
    return pl.pallas_call(
        finish_body,
        out_shape=[
            jax.ShapeDtypeStruct((CELL_DEV, D), F32),
            jax.ShapeDtypeStruct((CELL_DEV, D, D), F32),
        ],
        in_specs=[SMEM_SPEC] + [VMEM_SPEC] * NZ,
        out_specs=[VMEM_SPEC, VMEM_SPEC],
        compiler_params=pltpu.CompilerParams(vmem_limit_bytes=VMEM_LIMIT),
        name="finish",
    )(pos, *parts)


def local(vectors, block_cells, dest_counts):
    pos = place()
    counts, cells = dest_counts[0, 0], block_cells[0]
    rows = vectors.reshape(BLK * ROWS, D)
    sent, got = [], []
    for group, units in enumerate(UNITS):
        turn, flows, header = pos, [(d, units) for d in SHIFTS], ()
        if group == 0:
            flows, header = flows[1:], (block_cells, dest_counts[0])
        elif group == 1:
            turn, *_ = lax.optimization_barrier((pos, *sent[0]))
            flows = flows[1:]
        else:
            if group == 2:
                lists, sizes, tallies = make_lists(pos, cells, counts, got[0])
            turn, *_ = lax.optimization_barrier((pos, sizes, *got[group - 2][-3:]))
            flows = [(0, UNITS[group - 2])] + flows
        runs = gather_runs(flows, turn, counts, rows, f"gather{group}", header)
        sent.append(runs)
        if group > 1:
            got[group - 2].insert(0, runs[0])
        got.append(list(runs[1:-3]) + [lax.ppermute(run, "cell", along(d)) for d, run in zip(SHIFTS[1:], runs[-3:])])

    def step(rel, piece):
        return lax.ppermute(piece, "cell", across(rel))

    fore, back = gram(0, lists, sizes, tallies, got[0])
    fore, back = step(1, fore), step(3, back)
    left, right = gram(2, lists, sizes, tallies, got[2])
    other1, own3 = step(1, left), step(3, right)
    left, right = gram(3, lists, sizes, tallies, got[3], (fore,), (back,))
    own1, other3 = step(1, left), step(3, right)
    own, other = gram(1, lists, sizes, tallies, got[1], (own3,), (other1,))
    swapped = lax.ppermute(other_total([other, other3]), "cell", SWAP)
    quarters = join(pos, [own, own1, swapped])
    mine = quarters[0]
    for dz in range(1, NZ):
        mine = mine + lax.ppermute(quarters[dz], "dp", dp_perm(dz))
    whole = [mine] + [lax.ppermute(mine, "dp", dp_perm(dz)) for dz in range(1, NZ)]
    return tuple(finish(pos, whole))


def solution(mesh):
    in_specs = (P("dp", "cell", None, None), P("dp", "cell"), P("dp", "cell", None))
    out_specs = (P("cell", None), P("cell", None, None))
    return jax.shard_map(local, mesh=mesh, in_specs=in_specs, out_specs=out_specs, check_vma=False)
```

```python
import jax
import jax.numpy as jnp
from jax import lax
from jax.experimental import pallas as pl
from jax.experimental.pallas import tpu as pltpu
from jax.sharding import PartitionSpec as P

CELLS = 1024
NX = NY = NZ = 4
NC = 2
OWNERS = NX * NY * NC
CELL_DEV = CELLS // OWNERS
BLK = 384
ROWS = 64
D = 128
RUN = 24
SLOTS = NC * RUN
SHIFTS = (0, 1, 3, 2)
COPIES = 1
GROUPS = len(SHIFTS)
CHIP_CELLS = NC * CELL_DEV
LIST = 4 * GROUPS * SLOTS + 128
PAIR = 8
F32 = jnp.float32
I32 = jnp.int32
HEAD = 16
UNITS = (((2, 0), (2, 1)), ((0, 0), (0, 1)), ((1, 1), (3, 0)), ((1, 0), (3, 1)))
PACKED = CELL_DEV * ROWS
PIECE = PACKED + 3 * CELL_DEV
QCELL = CELL_DEV // NZ
QPACKED = QCELL * ROWS
QPIECE = QPACKED + 3 * QCELL
VMEM_LIMIT = 16 * 1024 * 1024
LARGE_VMEM = 56 * 1024 * 1024
SMALL_VMEM = 6 * 1024 * 1024

SMEM_SPEC = pl.BlockSpec(memory_space=pltpu.SMEM)
VMEM_SPEC = pl.BlockSpec(memory_space=pltpu.VMEM)
HBM_SPEC = pl.BlockSpec(memory_space=pltpu.HBM)


def at(x, y, c):
    return (x * NY + y) * NC + c


def cell_perm(even, odd, dc=0):
    steps = (even, odd)
    return [
        (at(x, y, c), at((x + steps[c][0]) % NX, (y + steps[c][1]) % NY, c ^ dc))
        for x in range(NX)
        for y in range(NY)
        for c in range(NC)
    ]


def along(d):
    return cell_perm((d, 0), (0, d))


def across(d):
    return cell_perm((0, d), (d, 0))


SWAP = cell_perm((0, 0), (0, 0), 1)


def dp_perm(dz):
    return [(z, (z + dz) % NZ) for z in range(NZ)]


def place():
    me = lax.axis_index("cell")
    x, y, c = me // (NY * NC), (me // NC) % NY, me % NC
    first, second = jnp.where(c == 0, x, y), jnp.where(c == 0, y, x)
    return jnp.stack([first, second, c, lax.axis_index("dp")]).astype(I32)


def owner(c, first, second, oc):
    return jnp.where(c == 0, at(first, second, oc), at(second, first, oc))


def unit_owner(pos, d, rel, side):
    return owner(pos[2], lax.rem(pos[0] + d, 4), lax.rem(pos[1] + rel, 4), lax.rem(pos[2] + side, 2))


def gather_body(flows, head, pos, counts, vectors, *refs):
    header, refs = (refs[:2], refs[2:]) if head else ((), refs)
    outs = refs[: len(flows)]
    offsets, sems = refs[len(flows) : len(flows) + 2]
    total = jnp.int32(0)
    for o in range(OWNERS):
        offsets[o] = total
        total = total + counts[o]
    copies = []
    rows = RUN * ROWS // COPIES
    for out, (d, units) in zip(outs, flows):
        for i, (rel, side) in enumerate(units):
            start = jnp.minimum(offsets[unit_owner(pos, d, rel, side)], BLK - RUN)
            for part in range(COPIES):
                copies.append(
                    pltpu.make_async_copy(
                        vectors.at[pl.ds(pl.multiple_of(start * ROWS + part * rows, ROWS), rows)],
                        out.at[pl.ds((i * COPIES + part) * rows, rows)],
                        sems.at[len(copies)],
                    )
                )
                copies[-1].start()
    if head:
        cells, count_row = header
        text = refs[-1]
        text[...] = jnp.zeros((HEAD, D), F32)
        for i in range(BLK // D):
            text[i : i + 1, :] = cells[:, i * D : (i + 1) * D].astype(F32)
        text[BLK // D : BLK // D + 1, :OWNERS] = count_row[...].astype(F32)
        for out in outs:
            out[pl.ds(SLOTS * ROWS, HEAD), :] = text[...].astype(out.dtype)
    for copy in copies:
        copy.wait()


def gather_runs(flows, pos, counts, vectors, name, header=()):
    def body(*refs):
        gather_body(flows, bool(header), *refs)

    rows = SLOTS * ROWS + (HEAD if header else 0)
    return pl.pallas_call(
        body,
        out_shape=[jax.ShapeDtypeStruct((rows, D), vectors.dtype)] * len(flows),
        in_specs=[SMEM_SPEC, SMEM_SPEC, HBM_SPEC] + [VMEM_SPEC] * len(header),
        out_specs=[VMEM_SPEC] * len(flows),
        scratch_shapes=[pltpu.SMEM((OWNERS,), I32), pltpu.SemaphoreType.DMA((2 * COPIES * len(flows),))]
        + ([pltpu.VMEM((HEAD, D), F32)] if header else []),
        compiler_params=pltpu.CompilerParams(vmem_limit_bytes=LARGE_VMEM if header else SMALL_VMEM),
        name=name,
    )(pos, counts, vectors, *header)


def lists_body(pos, own_cells, own_counts, *refs):
    heads = refs[: GROUPS - 1]
    lists, sizes, tallies, offsets, text, metas, sem = refs[GROUPS - 1 :]
    for g, head in enumerate(heads):
        text[pl.ds(g * 8, 8), :] = head[...].astype(F32)[:8].astype(I32)
    copy = pltpu.make_async_copy(text, metas, sem.at[0])
    copy.start()

    def clear(i, _):
        for u in range(8):
            tallies[i * 8 + u] = jnp.int32(0)
        return 0

    lax.fori_loop(0, 4 * CHIP_CELLS // 8, clear, 0)
    copy.wait()

    def count_of(g, o):
        return own_counts[o] if g == 0 else metas[(g - 1) * 8 + BLK // D, o]

    def cell_of(g, i):
        return own_cells[i] if g == 0 else metas[(g - 1) * 8 + (i >> 7), i & (D - 1)]

    for g in range(GROUPS):
        total = jnp.int32(0)
        for o in range(OWNERS):
            offsets[g * OWNERS + o] = total
            total = total + count_of(g, o)
    begin = jnp.int32(0)
    for group, units in enumerate(UNITS):
        for g in range(GROUPS):
            filled = begin
            for i, (rel, side) in enumerate(units):
                o = unit_owner(pos, 0, rel, side)
                n = count_of(g, o)
                start = offsets[g * OWNERS + o]
                slot = i * RUN + start - jnp.minimum(start, BLK - RUN)
                base = (slot << 17) + i * ((PIECE // 8 << 7) + CELL_DEV)
                tally = group * CHIP_CELLS + i * CELL_DEV

                def add(j, f, g=g, start=start, base=base, tally=tally):
                    cell = cell_of(g, start + j)
                    lists[f + j] = base + (j << 17) + cell * ((ROWS // 8 << 7) + 1)
                    tallies[tally + cell] = tallies[tally + cell] + ROWS
                    return f

                lax.fori_loop(0, n, add, filled)
                filled = filled + n
            for j in range(PAIR):
                lists[filled + j] = jnp.int32((PACKED // 8 << 7) + CHIP_CELLS)
            segment = group * GROUPS + g
            sizes[2 * segment] = begin
            sizes[2 * segment + 1] = (filled - begin + PAIR - 1) // PAIR
            begin = begin + sizes[2 * segment + 1] * PAIR


def make_lists(pos, own_cells, own_counts, arrived):
    head = pl.BlockSpec((HEAD, D), lambda i: (SLOTS * ROWS // HEAD, 0))
    return pl.pallas_call(
        lists_body,
        out_shape=[
            jax.ShapeDtypeStruct((LIST,), I32),
            jax.ShapeDtypeStruct((8 * GROUPS,), I32),
            jax.ShapeDtypeStruct((4 * CHIP_CELLS,), I32),
        ],
        grid=(1,),
        in_specs=[SMEM_SPEC] * 3 + [head] * (GROUPS - 1),
        out_specs=[SMEM_SPEC] * 3,
        scratch_shapes=[
            pltpu.SMEM((GROUPS * OWNERS,), I32),
            pltpu.VMEM(((GROUPS - 1) * 8, D), I32),
            pltpu.SMEM(((GROUPS - 1) * 8, D), I32),
            pltpu.SemaphoreType.DMA((1,)),
        ],
        compiler_params=pltpu.CompilerParams(vmem_limit_bytes=SMALL_VMEM),
        name="lists",
    )(pos, own_cells, own_counts, *arrived)


def add_blocks(segment, lists, sizes, buf, acc, acc_s, acc_q):
    begin, steps = sizes[2 * segment], sizes[2 * segment + 1]
    row = lax.broadcasted_iota(I32, (ROWS, D), 0)
    lane = lax.broadcasted_iota(I32, (ROWS, D), 1)
    upper = lane >= row
    contract = (((0,), (0,)), ((), ()))

    def step(i, _):
        done = []
        for u in range(PAIR):
            entry = lists[begin + i * PAIR + u]
            block = buf[pl.ds(pl.multiple_of((entry >> 17) * ROWS, ROWS), ROWS), :]
            turned = jnp.concatenate([block[:, ROWS:], block[:, :ROWS]], axis=1)
            top = lax.dot_general(block[:, :ROWS], block, contract, preferred_element_type=F32)
            low = lax.dot_general(block[:, ROWS:], turned, contract, preferred_element_type=F32)
            wide = block.astype(F32)
            done.append(
                (
                    pl.multiple_of(((entry >> 7) & 1023) * 8, 8),
                    pl.multiple_of((entry & 127) * 8, 8),
                    jnp.where(upper, top, low),
                    jnp.sum(wide.reshape(8, 8, D), axis=0),
                    jnp.sum((wide * wide).reshape(8, 8, D), axis=0),
                )
            )
        for at_row, at_sum, gram, total, square in done:
            here, near = pl.ds(at_row, ROWS), pl.ds(at_sum, 8)
            acc[here, :] = acc[here, :] + gram
            acc_s[near, :] = acc_s[near, :] + total
            acc_q[near, :] = acc_q[near, :] + square
        return 0

    lax.fori_loop(0, steps, step, 0)


def gram_body(group, members, counted, quartered, started, pos, lists, sizes, tallies, *refs):
    blocks, refs = refs[: len(members)], refs[len(members) :]
    first, second = started
    starts = (refs[:first], refs[first : first + second])
    outs, (acc, acc_s, acc_q) = refs[first + second : -3], refs[-3:]

    def add_starts(value, u, rows):
        for start in starts[u]:
            value = value + start[rows, :]
        return value

    def clear(i, _):
        rows = pl.ds(pl.multiple_of(i * ROWS, ROWS), ROWS)
        for u in range(2):
            value = add_starts(jnp.zeros((ROWS, D), F32), u, rows)
            acc[pl.ds(pl.multiple_of(u * PIECE + i * ROWS, 8), ROWS), :] = value
        return 0

    lax.fori_loop(0, CELL_DEV, clear, 0)

    def clear_sums(i, _):
        acc_s[pl.ds(pl.multiple_of(i * 8, 8), 8), :] = jnp.zeros((8, D), F32)
        acc_q[pl.ds(pl.multiple_of(i * 8, 8), 8), :] = jnp.zeros((8, D), F32)
        return 0

    lax.fori_loop(0, CHIP_CELLS, clear_sums, 0)
    for g, member in zip(members, blocks):
        add_blocks(group * GROUPS + g, lists, sizes, member, acc, acc_s, acc_q)
    for u in range(2):
        base = u * PIECE
        for k, source in enumerate((acc_s, acc_q)):
            total = source[pl.ds(u * CELL_DEV * 8, CELL_DEV, stride=8), :]
            for j in range(1, 8):
                total = total + source[pl.ds(u * CELL_DEV * 8 + j, CELL_DEV, stride=8), :]
            rows = PACKED + k * CELL_DEV
            acc[pl.ds(base + rows, CELL_DEV), :] = add_starts(total, u, pl.ds(rows, CELL_DEV))
        for j in range(CELL_DEV):
            count = jnp.zeros((1, D), F32)
            if counted:
                count = jnp.full((1, D), tallies[group * CHIP_CELLS + u * CELL_DEV + j].astype(F32), F32)
            rows = PACKED + 2 * CELL_DEV + j
            acc[pl.ds(base + rows, 1), :] = add_starts(count, u, pl.ds(rows, 1))
    if not quartered:

        def copy_out(i, _):
            for u in range(2):
                outs[u][pl.ds(pl.multiple_of(i * 32, 32), 32), :] = acc[
                    pl.ds(pl.multiple_of(u * PIECE + i * 32, 32), 32), :
                ]
            return 0

        lax.fori_loop(0, PIECE // 32, copy_out, 0)
        return
    for dz in range(NZ):
        q = lax.rem(pos[3] + dz, NZ)
        for u in range(2):

            def copy_quarter(i, _, dz=dz, q=q, u=u):
                outs[dz][pl.ds(pl.multiple_of(u * QPIECE + i * ROWS, 8), ROWS), :] = acc[
                    pl.ds(pl.multiple_of(u * PIECE + q * QPACKED + i * ROWS, 8), ROWS), :
                ]
                return 0

            lax.fori_loop(0, QCELL, copy_quarter, 0)
            for k in range(3):
                outs[dz][pl.ds(u * QPIECE + QPACKED + k * QCELL, QCELL), :] = acc[
                    pl.ds(pl.multiple_of(u * PIECE + PACKED + k * CELL_DEV + q * QCELL, QCELL), QCELL), :
                ]


def gram(group, pos, lists, sizes, tallies, blocks, first=(), second=(), members=(0, 1, 2, 3), counted=True, quartered=False):
    def body(*refs):
        gram_body(group, members, counted, quartered, (len(first), len(second)), *refs)

    half = jax.ShapeDtypeStruct((PIECE, D), F32)
    quarter = jax.ShapeDtypeStruct((2 * QPIECE, D), F32)
    outs = [quarter] * NZ if quartered else [half] * 2
    return pl.pallas_call(
        body,
        out_shape=outs,
        in_specs=[SMEM_SPEC] * 4 + [VMEM_SPEC] * (len(members) + len(first) + len(second)),
        out_specs=[VMEM_SPEC] * len(outs),
        scratch_shapes=[pltpu.VMEM((NC * PIECE, D), F32)] + [pltpu.VMEM(((CHIP_CELLS + 1) * 8, D), F32)] * 2,
        compiler_params=pltpu.CompilerParams(vmem_limit_bytes=SMALL_VMEM),
        cost_estimate=pl.CostEstimate(flops=10**9, bytes_accessed=10**7, transcendentals=0),
        name=f"gram{group}" + ("" if counted else "b"),
    )(pos, lists, sizes, tallies, *(blocks[g] for g in members), *first, *second)


def total_body(*refs):
    def step(i, _):
        rows = pl.ds(pl.multiple_of(i * 32, 32), 32)
        value = refs[0][rows, :]
        for part in refs[1:-1]:
            value = value + part[rows, :]
        refs[-1][rows, :] = value
        return 0

    lax.fori_loop(0, PIECE // 32, step, 0)


def other_total(parts):
    return pl.pallas_call(
        total_body,
        out_shape=jax.ShapeDtypeStruct((PIECE, D), F32),
        in_specs=[VMEM_SPEC] * len(parts),
        out_specs=VMEM_SPEC,
        compiler_params=pltpu.CompilerParams(vmem_limit_bytes=SMALL_VMEM),
        name="other_total",
    )(*parts)


def join_body(extra, pos, *refs):
    outs, parts = refs[-NZ:], refs[:-NZ]
    parts, extras = parts[: len(parts) - extra], parts[len(parts) - extra :]
    z = pos[3]

    def total(rows):
        value = parts[0][rows, :]
        for part in parts[1:]:
            value = value + part[rows, :]
        return value

    for dz in range(NZ):
        q = lax.rem(z + dz, NZ)

        def put(rows, value, dz=dz):
            for more in extras if dz == 0 else ():
                value = value + more[rows, :]
            outs[dz][rows, :] = value

        def step(i, _, q=q, put=put):
            put(
                pl.ds(pl.multiple_of(i * ROWS, ROWS), ROWS),
                total(pl.ds(pl.multiple_of(q * QPACKED + i * ROWS, ROWS), ROWS)),
            )
            return 0

        lax.fori_loop(0, QCELL, step, 0)
        for k in range(3):
            put(
                pl.ds(QPACKED + k * QCELL, QCELL),
                total(pl.ds(pl.multiple_of(PACKED + k * CELL_DEV + q * QCELL, QCELL), QCELL)),
            )


def join(pos, parts, extras=()):
    def body(*refs):
        join_body(len(extras), *refs)

    return pl.pallas_call(
        body,
        out_shape=[jax.ShapeDtypeStruct((QPIECE, D), F32)] * NZ,
        in_specs=[SMEM_SPEC] + [VMEM_SPEC] * (len(parts) + len(extras)),
        out_specs=[VMEM_SPEC] * NZ,
        compiler_params=pltpu.CompilerParams(vmem_limit_bytes=SMALL_VMEM),
        name="join",
    )(pos, *parts, *extras)


def finish_body(pos, *refs):
    parts = refs[:NZ]
    mean_out, cov_out = refs[NZ:]
    z = pos[3]
    row = lax.broadcasted_iota(I32, (ROWS, D), 0)
    lane = lax.broadcasted_iota(I32, (ROWS, D), 1)
    for dz in range(NZ):
        q = lax.rem(z + NZ - dz, NZ)
        part = parts[dz]
        sums = part[pl.ds(QPACKED, QCELL), :]
        counts = part[pl.ds(QPACKED + 2 * QCELL, QCELL), :]
        safe = jnp.maximum(counts, 1.0)
        mean = sums / safe
        inverse = 1.0 / safe
        mean_out[pl.ds(pl.multiple_of(q * QCELL, QCELL), QCELL), :] = mean
        scaled = jnp.transpose(jnp.concatenate([mean * counts] * (D // QCELL), axis=0))
        for j in range(QCELL):
            packed = part[pl.ds(j * ROWS, ROWS), :]
            diagonal = part[pl.ds(QPACKED + QCELL + j, 1), :]
            flipped = jnp.transpose(jnp.concatenate([packed, packed], axis=0))
            rolled = pltpu.roll(packed, ROWS, 1)
            high, low = flipped[:ROWS], flipped[ROWS:]
            top = jnp.where(lane >= row, packed, high)
            corner = jnp.where(lane - ROWS < row, rolled, jnp.where(lane - ROWS == row, diagonal, high))
            bottom = jnp.where(lane < ROWS, low, corner)
            full = jnp.concatenate([top, bottom], axis=0)
            outer = scaled[:, j : j + 1] * mean[j : j + 1, :]
            cov_out[q * QCELL + j] = (full - outer) * inverse[j : j + 1, :]


def finish(pos, parts):
    return pl.pallas_call(
        finish_body,
        out_shape=[
            jax.ShapeDtypeStruct((CELL_DEV, D), F32),
            jax.ShapeDtypeStruct((CELL_DEV, D, D), F32),
        ],
        in_specs=[SMEM_SPEC] + [VMEM_SPEC] * NZ,
        out_specs=[VMEM_SPEC, VMEM_SPEC],
        compiler_params=pltpu.CompilerParams(vmem_limit_bytes=VMEM_LIMIT),
        name="finish",
    )(pos, *parts)


def local(vectors, block_cells, dest_counts):
    pos = place()
    counts, cells = dest_counts[0, 0], block_cells[0]
    rows = vectors.reshape(BLK * ROWS, D)
    sent, got = [], []
    for group, units in enumerate(UNITS):
        turn, flows, header = pos, [(d, units) for d in SHIFTS], ()
        if group == 0:
            flows, header = flows[1:], (block_cells, dest_counts[0])
        elif group == 1:
            turn, *_ = lax.optimization_barrier((pos, *sent[0]))
            flows = flows[1:]
        else:
            if group == 2:
                lists, sizes, tallies = make_lists(pos, cells, counts, got[0])
            turn, *_ = lax.optimization_barrier((pos, sizes, *got[group - 2][-3:]))
            flows = [(0, UNITS[group - 2])] + flows
        runs = gather_runs(flows, turn, counts, rows, f"gather{group}", header)
        sent.append(runs)
        if group > 1:
            got[group - 2].insert(0, runs[0])
        got.append(list(runs[1:-3]) + [lax.ppermute(run, "cell", along(d)) for d, run in zip(SHIFTS[1:], runs[-3:])])

    def step(rel, piece):
        return lax.ppermute(piece, "cell", across(rel))

    def grams(group, *rest, **options):
        return gram(group, pos, lists, sizes, tallies, got[group], *rest, **options)

    fore, back = grams(0)
    fore, back = step(1, fore), step(3, back)
    left, right = grams(2)
    other1, own3 = step(1, left), step(3, right)
    left, right = grams(3, (fore,), (back,), members=(0, 1))
    left, right = grams(3, (left,), (right,), members=(2, 3), counted=False)
    own1, other3 = step(1, left), step(3, right)
    own, other = grams(1, (own3,), (other1,))
    swapped = lax.ppermute(other_total([other, other3]), "cell", SWAP)
    quarters = join(pos, [own, own1, swapped])
    mine = quarters[0]
    for dz in range(1, NZ):
        mine = mine + lax.ppermute(quarters[dz], "dp", dp_perm(dz))
    whole = [mine] + [lax.ppermute(mine, "dp", dp_perm(dz)) for dz in range(1, NZ)]
    return tuple(finish(pos, whole))


def solution(mesh):
    in_specs = (P("dp", "cell", None, None), P("dp", "cell"), P("dp", "cell", None))
    out_specs = (P("cell", None), P("cell", None, None))
    return jax.shard_map(local, mesh=mesh, in_specs=in_specs, out_specs=out_specs, check_vma=False)
```

```python
import jax
import jax.numpy as jnp
from jax import lax
from jax.experimental import pallas as pl
from jax.experimental.pallas import tpu as pltpu
from jax.sharding import PartitionSpec as P

CELLS = 1024
NX = NY = NZ = 4
NC = 2
OWNERS = NX * NY * NC
CELL_DEV = CELLS // OWNERS
BLK = 384
ROWS = 64
D = 128
RUN = 24
SLOTS = NC * RUN
SHIFTS = (0, 1, 3, 2)
COPIES = 1
GROUPS = len(SHIFTS)
CHIP_CELLS = NC * CELL_DEV
LIST = 4 * GROUPS * SLOTS + 128
PAIR = 8
F32 = jnp.float32
I32 = jnp.int32
HEAD = 16
UNITS = (((2, 0), (2, 1)), ((0, 0), (0, 1)), ((1, 1), (3, 0)), ((1, 0), (3, 1)))
PACKED = (CELL_DEV - 1) * ROWS
PIECE = PACKED + 2 * CELL_DEV
QCELL = CELL_DEV // NZ
QPACKED = QCELL * ROWS
QPIECE = QPACKED + 2 * QCELL
VMEM_LIMIT = 16 * 1024 * 1024
LARGE_VMEM = 56 * 1024 * 1024
SMALL_VMEM = 6 * 1024 * 1024

SMEM_SPEC = pl.BlockSpec(memory_space=pltpu.SMEM)
VMEM_SPEC = pl.BlockSpec(memory_space=pltpu.VMEM)
HBM_SPEC = pl.BlockSpec(memory_space=pltpu.HBM)


def at(x, y, c):
    return (x * NY + y) * NC + c


def cell_perm(even, odd, dc=0):
    steps = (even, odd)
    return [
        (at(x, y, c), at((x + steps[c][0]) % NX, (y + steps[c][1]) % NY, c ^ dc))
        for x in range(NX)
        for y in range(NY)
        for c in range(NC)
    ]


def along(d):
    return cell_perm((d, 0), (0, d))


def across(d):
    return cell_perm((0, d), (d, 0))


SWAP = cell_perm((0, 0), (0, 0), 1)


def dp_perm(dz):
    return [(z, (z + dz) % NZ) for z in range(NZ)]


def place():
    me = lax.axis_index("cell")
    x, y, c = me // (NY * NC), (me // NC) % NY, me % NC
    first, second = jnp.where(c == 0, x, y), jnp.where(c == 0, y, x)
    return jnp.stack([first, second, c, lax.axis_index("dp")]).astype(I32)


def owner(c, first, second, oc):
    return jnp.where(c == 0, at(first, second, oc), at(second, first, oc))


def unit_owner(pos, d, rel, side):
    return owner(pos[2], lax.rem(pos[0] + d, 4), lax.rem(pos[1] + rel, 4), lax.rem(pos[2] + side, 2))


def gather_body(flows, head, pos, counts, vectors, *refs):
    header, refs = (refs[:2], refs[2:]) if head else ((), refs)
    outs = refs[: len(flows)]
    offsets, sems = refs[len(flows) : len(flows) + 2]
    total = jnp.int32(0)
    for o in range(OWNERS):
        offsets[o] = total
        total = total + counts[o]
    copies = []
    rows = RUN * ROWS // COPIES
    for out, (d, units) in zip(outs, flows):
        for i, (rel, side) in enumerate(units):
            start = jnp.minimum(offsets[unit_owner(pos, d, rel, side)], BLK - RUN)
            for part in range(COPIES):
                copies.append(
                    pltpu.make_async_copy(
                        vectors.at[pl.ds(pl.multiple_of(start * ROWS + part * rows, ROWS), rows)],
                        out.at[pl.ds((i * COPIES + part) * rows, rows)],
                        sems.at[len(copies)],
                    )
                )
                copies[-1].start()
    if head:
        cells, count_row = header
        text = refs[-1]
        text[...] = jnp.zeros((HEAD, D), F32)
        for i in range(BLK // D):
            text[i : i + 1, :] = cells[:, i * D : (i + 1) * D].astype(F32)
        text[BLK // D : BLK // D + 1, :OWNERS] = count_row[...].astype(F32)
        for out in outs:
            out[pl.ds(SLOTS * ROWS, HEAD), :] = text[...].astype(out.dtype)
    for copy in copies:
        copy.wait()


def gather_runs(flows, pos, counts, vectors, name, header=()):
    def body(*refs):
        gather_body(flows, bool(header), *refs)

    rows = SLOTS * ROWS + (HEAD if header else 0)
    return pl.pallas_call(
        body,
        out_shape=[jax.ShapeDtypeStruct((rows, D), vectors.dtype)] * len(flows),
        in_specs=[SMEM_SPEC, SMEM_SPEC, HBM_SPEC] + [VMEM_SPEC] * len(header),
        out_specs=[VMEM_SPEC] * len(flows),
        scratch_shapes=[pltpu.SMEM((OWNERS,), I32), pltpu.SemaphoreType.DMA((2 * COPIES * len(flows),))]
        + ([pltpu.VMEM((HEAD, D), F32)] if header else []),
        compiler_params=pltpu.CompilerParams(vmem_limit_bytes=LARGE_VMEM if header else SMALL_VMEM),
        name=name,
    )(pos, counts, vectors, *header)


def lists_body(pos, own_cells, own_counts, *refs):
    heads = refs[: GROUPS - 1]
    lists, sizes, tallies, offsets, text, metas, sem = refs[GROUPS - 1 :]
    for g, head in enumerate(heads):
        text[pl.ds(g * 8, 8), :] = head[...].astype(F32)[:8].astype(I32)
    copy = pltpu.make_async_copy(text, metas, sem.at[0])
    copy.start()

    def clear(i, _):
        for u in range(8):
            tallies[i * 8 + u] = jnp.int32(0)
        return 0

    lax.fori_loop(0, 4 * CHIP_CELLS // 8, clear, 0)
    copy.wait()

    def count_of(g, o):
        return own_counts[o] if g == 0 else metas[(g - 1) * 8 + BLK // D, o]

    def cell_of(g, i):
        return own_cells[i] if g == 0 else metas[(g - 1) * 8 + (i >> 7), i & (D - 1)]

    for g in range(GROUPS):
        total = jnp.int32(0)
        for o in range(OWNERS):
            offsets[g * OWNERS + o] = total
            total = total + count_of(g, o)
    begin = jnp.int32(0)
    for group, units in enumerate(UNITS):
        for g in range(GROUPS):
            filled = begin
            for i, (rel, side) in enumerate(units):
                o = unit_owner(pos, 0, rel, side)
                n = count_of(g, o)
                start = offsets[g * OWNERS + o]
                slot = i * RUN + start - jnp.minimum(start, BLK - RUN)
                base = (slot << 17) + i * ((PIECE // 8 << 7) + CELL_DEV)
                tally = group * CHIP_CELLS + i * CELL_DEV

                def add(j, f, g=g, start=start, base=base, tally=tally):
                    cell = cell_of(g, start + j)
                    lists[f + j] = base + (j << 17) + cell * ((ROWS // 8 << 7) + 1)
                    tallies[tally + cell] = tallies[tally + cell] + ROWS
                    return f

                lax.fori_loop(0, n, add, filled)
                filled = filled + n
            for j in range(PAIR):
                lists[filled + j] = jnp.int32((PACKED // 8 << 7) + CHIP_CELLS)
            segment = group * GROUPS + g
            sizes[2 * segment] = begin
            sizes[2 * segment + 1] = (filled - begin + PAIR - 1) // PAIR
            begin = begin + sizes[2 * segment + 1] * PAIR


def make_lists(pos, own_cells, own_counts, arrived):
    head = pl.BlockSpec((HEAD, D), lambda i: (SLOTS * ROWS // HEAD, 0))
    return pl.pallas_call(
        lists_body,
        out_shape=[
            jax.ShapeDtypeStruct((LIST,), I32),
            jax.ShapeDtypeStruct((8 * GROUPS,), I32),
            jax.ShapeDtypeStruct((4 * CHIP_CELLS,), I32),
        ],
        grid=(1,),
        in_specs=[SMEM_SPEC] * 3 + [head] * (GROUPS - 1),
        out_specs=[SMEM_SPEC] * 3,
        scratch_shapes=[
            pltpu.SMEM((GROUPS * OWNERS,), I32),
            pltpu.VMEM(((GROUPS - 1) * 8, D), I32),
            pltpu.SMEM(((GROUPS - 1) * 8, D), I32),
            pltpu.SemaphoreType.DMA((1,)),
        ],
        compiler_params=pltpu.CompilerParams(vmem_limit_bytes=SMALL_VMEM),
        name="lists",
    )(pos, own_cells, own_counts, *arrived)


def add_blocks(segment, lists, sizes, buf, acc, acc_s, acc_q):
    begin, steps = sizes[2 * segment], sizes[2 * segment + 1]
    row = lax.broadcasted_iota(I32, (ROWS, D), 0)
    lane = lax.broadcasted_iota(I32, (ROWS, D), 1)
    upper = lane >= row
    contract = (((0,), (0,)), ((), ()))

    def step(i, _):
        done = []
        for u in range(PAIR):
            entry = lists[begin + i * PAIR + u]
            block = buf[pl.ds(pl.multiple_of((entry >> 17) * ROWS, ROWS), ROWS), :]
            turned = jnp.concatenate([block[:, ROWS:], block[:, :ROWS]], axis=1)
            top = lax.dot_general(block[:, :ROWS], block, contract, preferred_element_type=F32)
            low = lax.dot_general(block[:, ROWS:], turned, contract, preferred_element_type=F32)
            wide = block.astype(F32)
            done.append(
                (
                    pl.multiple_of(((entry >> 7) & 1023) * 8, 8),
                    pl.multiple_of((entry & 127) * 8, 8),
                    jnp.where(upper, top, low),
                    jnp.sum(wide.reshape(8, 8, D), axis=0),
                    jnp.sum((wide * wide).reshape(8, 8, D), axis=0),
                )
            )
        for at_row, at_sum, gram, total, square in done:
            here, near = pl.ds(at_row, ROWS), pl.ds(at_sum, 8)
            acc[here, :] = acc[here, :] + gram
            acc_s[near, :] = acc_s[near, :] + total
            acc_q[near, :] = acc_q[near, :] + square
        return 0

    lax.fori_loop(0, steps, step, 0)


def gram_body(group, members, counted, started, lists, sizes, tallies, *refs):
    blocks, refs = refs[: len(members)], refs[len(members) :]
    first, second = started
    starts = (refs[:first], refs[first : first + second])
    outs, (acc, acc_s, acc_q) = refs[first + second : -3], refs[-3:]

    def add_starts(value, u, rows):
        for start in starts[u]:
            value = value + start[rows, :]
        return value

    def clear(i, _):
        rows = pl.ds(pl.multiple_of(i * ROWS, ROWS), ROWS)
        for u in range(2):
            value = add_starts(jnp.zeros((ROWS, D), F32), u, rows)
            acc[pl.ds(pl.multiple_of(u * PIECE + i * ROWS, 8), ROWS), :] = value
        return 0

    lax.fori_loop(0, PACKED // ROWS, clear, 0)

    def clear_sums(i, _):
        acc_s[pl.ds(pl.multiple_of(i * 8, 8), 8), :] = jnp.zeros((8, D), F32)
        acc_q[pl.ds(pl.multiple_of(i * 8, 8), 8), :] = jnp.zeros((8, D), F32)
        return 0

    lax.fori_loop(0, CHIP_CELLS, clear_sums, 0)
    for g, member in zip(members, blocks):
        add_blocks(group * GROUPS + g, lists, sizes, member, acc, acc_s, acc_q)
    lane = lax.broadcasted_iota(I32, (CELL_DEV, D), 1)
    for u in range(2):
        totals = []
        for source in (acc_s, acc_q):
            total = source[pl.ds(u * CELL_DEV * 8, CELL_DEV, stride=8), :]
            for j in range(1, 8):
                total = total + source[pl.ds(u * CELL_DEV * 8 + j, CELL_DEV, stride=8), :]
            totals.append(total)
        count = jnp.zeros((CELL_DEV, D), F32)
        if counted:
            for j in range(CELL_DEV):
                value = tallies[group * CHIP_CELLS + u * CELL_DEV + j].astype(F32)
                acc_s[pl.ds(u * CELL_DEV * 8 + j, 1), :] = jnp.full((1, D), value, F32)
            count = acc_s[pl.ds(u * CELL_DEV * 8, CELL_DEV), :]
        totals[1] = jnp.where(lane < ROWS, count, totals[1])
        for k, total in enumerate(totals):
            rows = PACKED + k * CELL_DEV
            acc[pl.ds(u * PIECE + rows, CELL_DEV), :] = add_starts(total, u, pl.ds(rows, CELL_DEV))

    def copy_out(i, _):
        for u in range(2):
            outs[u][pl.ds(pl.multiple_of(i * 32, 32), 32), :] = acc[
                pl.ds(pl.multiple_of(u * PIECE + i * 32, 32), 32), :
            ]
        return 0

    lax.fori_loop(0, PIECE // 32, copy_out, 0)


def gram(group, lists, sizes, tallies, blocks, first=(), second=(), members=(0, 1, 2, 3), counted=True):
    def body(*refs):
        gram_body(group, members, counted, (len(first), len(second)), *refs)

    half = jax.ShapeDtypeStruct((PIECE, D), F32)
    outs = [half] * 2
    return pl.pallas_call(
        body,
        out_shape=outs,
        in_specs=[SMEM_SPEC] * 3 + [VMEM_SPEC] * (len(members) + len(first) + len(second)),
        out_specs=[VMEM_SPEC] * len(outs),
        scratch_shapes=[pltpu.VMEM((NC * PIECE, D), F32)] + [pltpu.VMEM(((CHIP_CELLS + 1) * 8, D), F32)] * 2,
        compiler_params=pltpu.CompilerParams(vmem_limit_bytes=SMALL_VMEM),
        cost_estimate=pl.CostEstimate(flops=10**9, bytes_accessed=10**7, transcendentals=0),
        name=f"gram{group}" + ("" if counted else "b"),
    )(lists, sizes, tallies, *(blocks[g] for g in members), *first, *second)


def total_body(*refs):
    def step(i, _):
        rows = pl.ds(pl.multiple_of(i * 32, 32), 32)
        value = refs[0][rows, :]
        for part in refs[1:-1]:
            value = value + part[rows, :]
        refs[-1][rows, :] = value
        return 0

    lax.fori_loop(0, PIECE // 32, step, 0)


def other_total(parts):
    return pl.pallas_call(
        total_body,
        out_shape=jax.ShapeDtypeStruct((PIECE, D), F32),
        in_specs=[VMEM_SPEC] * len(parts),
        out_specs=VMEM_SPEC,
        compiler_params=pltpu.CompilerParams(vmem_limit_bytes=SMALL_VMEM),
        name="other_total",
    )(*parts)


def join_body(pos, *refs):
    outs, parts = refs[-NZ:], refs[:-NZ]
    z = pos[3]

    def total(rows):
        value = parts[0][rows, :]
        for part in parts[1:]:
            value = value + part[rows, :]
        return value

    for dz in range(NZ):
        q = lax.rem(z + dz, NZ)

        def put(rows, value, dz=dz):
            outs[dz][rows, :] = value

        def step(i, _, q=q, put=put):
            put(
                pl.ds(pl.multiple_of(i * ROWS, ROWS), ROWS),
                total(pl.ds(pl.multiple_of(q * QPACKED + i * ROWS, ROWS), ROWS)),
            )
            return 0

        lax.fori_loop(0, QCELL, step, 0)
        for k in range(2):
            put(
                pl.ds(QPACKED + k * QCELL, QCELL),
                total(pl.ds(pl.multiple_of(PACKED + k * CELL_DEV + q * QCELL, QCELL), QCELL)),
            )


def join(pos, parts):
    return pl.pallas_call(
        join_body,
        out_shape=[jax.ShapeDtypeStruct((QPIECE, D), F32)] * NZ,
        in_specs=[SMEM_SPEC] + [VMEM_SPEC] * len(parts),
        out_specs=[VMEM_SPEC] * NZ,
        compiler_params=pltpu.CompilerParams(vmem_limit_bytes=SMALL_VMEM),
        name="join",
    )(pos, *parts)


def finish_body(pos, *refs):
    parts = refs[:NZ]
    mean_out, cov_out = refs[NZ:]
    z = pos[3]
    row = lax.broadcasted_iota(I32, (ROWS, D), 0)
    lane = lax.broadcasted_iota(I32, (ROWS, D), 1)
    for dz in range(NZ):
        q = lax.rem(z + NZ - dz, NZ)
        part = parts[dz]
        sums = part[pl.ds(QPACKED, QCELL), :]
        counts = jnp.broadcast_to(part[pl.ds(QPACKED + QCELL, QCELL), :][:, :1], (QCELL, D))
        safe = jnp.maximum(counts, 1.0)
        mean = sums / safe
        inverse = jnp.where(counts > 0.0, 1.0 / safe, 0.0)
        mean_out[pl.ds(pl.multiple_of(q * QCELL, QCELL), QCELL), :] = mean
        scaled = jnp.transpose(jnp.concatenate([mean * counts] * (D // QCELL), axis=0))
        for j in range(QCELL):
            packed = part[pl.ds(j * ROWS, ROWS), :]
            diagonal = part[pl.ds(QPACKED + QCELL + j, 1), :]
            flipped = jnp.transpose(jnp.concatenate([packed, packed], axis=0))
            rolled = pltpu.roll(packed, ROWS, 1)
            high, low = flipped[:ROWS], flipped[ROWS:]
            top = jnp.where(lane >= row, packed, high)
            corner = jnp.where(lane - ROWS < row, rolled, jnp.where(lane - ROWS == row, diagonal, high))
            bottom = jnp.where(lane < ROWS, low, corner)
            full = jnp.concatenate([top, bottom], axis=0)
            outer = scaled[:, j : j + 1] * mean[j : j + 1, :]
            cov_out[q * QCELL + j] = (full - outer) * inverse[j : j + 1, :]


def finish(pos, parts):
    return pl.pallas_call(
        finish_body,
        out_shape=[
            jax.ShapeDtypeStruct((CELL_DEV, D), F32),
            jax.ShapeDtypeStruct((CELL_DEV, D, D), F32),
        ],
        in_specs=[SMEM_SPEC] + [VMEM_SPEC] * NZ,
        out_specs=[VMEM_SPEC, VMEM_SPEC],
        compiler_params=pltpu.CompilerParams(vmem_limit_bytes=VMEM_LIMIT),
        name="finish",
    )(pos, *parts)


def local(vectors, block_cells, dest_counts):
    pos = place()
    counts, cells = dest_counts[0, 0], block_cells[0]
    rows = pltpu.with_memory_space_constraint(vectors.reshape(BLK * ROWS, D), pltpu.HBM)
    sent, got = [], []
    for group, units in enumerate(UNITS):
        turn, flows, header = pos, [(d, units) for d in SHIFTS], ()
        if group == 0:
            flows, header = flows[1:], (block_cells, dest_counts[0])
        elif group == 1:
            turn, *_ = lax.optimization_barrier((pos, *sent[0]))
            flows = flows[1:]
        else:
            if group == 2:
                lists, sizes, tallies = make_lists(pos, cells, counts, got[0])
            turn, *_ = lax.optimization_barrier((pos, sizes, *got[group - 2][-3:]))
            flows = [(0, UNITS[group - 2])] + flows
        runs = gather_runs(flows, turn, counts, rows, f"gather{group}", header)
        sent.append(runs)
        if group > 1:
            got[group - 2].insert(0, runs[0])
        got.append(list(runs[1:-3]) + [lax.ppermute(run, "cell", along(d)) for d, run in zip(SHIFTS[1:], runs[-3:])])

    def step(rel, piece):
        return lax.ppermute(piece, "cell", across(rel))

    def grams(group, *rest, **options):
        return gram(group, lists, sizes, tallies, got[group], *rest, **options)

    fore, back = grams(0)
    fore, back = step(1, fore), step(3, back)
    left, right = grams(2)
    other1, own3 = step(1, left), step(3, right)
    left, right = grams(3, (fore,), (back,), members=(0, 1))
    left, right = grams(3, (left,), (right,), members=(2, 3), counted=False)
    own1, other3 = step(1, left), step(3, right)
    own, other = grams(1, (own3,), (other1,))
    swapped = lax.ppermute(other_total([other, other3]), "cell", SWAP)
    quarters = join(pos, [own, own1, swapped])
    mine = quarters[0]
    for dz in range(1, NZ):
        mine = mine + lax.ppermute(quarters[dz], "dp", dp_perm(dz))
    whole = [mine] + [lax.ppermute(mine, "dp", dp_perm(dz)) for dz in range(1, NZ)]
    return tuple(finish(pos, whole))


def solution(mesh):
    in_specs = (P("dp", "cell", None, None), P("dp", "cell"), P("dp", "cell", None))
    out_specs = (P("cell", None), P("cell", None, None))
    return jax.shard_map(local, mesh=mesh, in_specs=in_specs, out_specs=out_specs, check_vma=False)
```

```python
import jax
import jax.numpy as jnp
from jax import lax
from jax.experimental import pallas as pl
from jax.experimental.pallas import tpu as pltpu
from jax.sharding import PartitionSpec as P

CELLS = 1024
NX = NY = NZ = 4
NC = 2
OWNERS = NX * NY * NC
CELL_DEV = CELLS // OWNERS
BLK = 384
ROWS = 64
D = 128
RUN = 24
SLOTS = NC * RUN
SHIFTS = (0, 1, 3, 2)
Z_SHIFTS = (1, 3, 2)
COPIES = 1
GROUPS = len(SHIFTS)
CHIP_CELLS = NC * CELL_DEV
LIST = 4 * GROUPS * SLOTS + 128
PAIR = 8
F32 = jnp.float32
I32 = jnp.int32
HEAD = 16
UNITS = (((2, 0), (2, 1)), ((0, 0), (0, 1)), ((1, 1), (3, 0)), ((1, 0), (3, 1)))
PACKED = (CELL_DEV - 1) * ROWS
PIECE = PACKED + 2 * CELL_DEV
QCELL = CELL_DEV // NZ
QPACKED = QCELL * ROWS
QPIECE = QPACKED + 2 * QCELL
VMEM_LIMIT = 16 * 1024 * 1024
LARGE_VMEM = 56 * 1024 * 1024
SMALL_VMEM = 6 * 1024 * 1024

SMEM_SPEC = pl.BlockSpec(memory_space=pltpu.SMEM)
VMEM_SPEC = pl.BlockSpec(memory_space=pltpu.VMEM)
HBM_SPEC = pl.BlockSpec(memory_space=pltpu.HBM)


def at(x, y, c):
    return (x * NY + y) * NC + c


def cell_perm(even, odd, dc=0):
    steps = (even, odd)
    return [
        (at(x, y, c), at((x + steps[c][0]) % NX, (y + steps[c][1]) % NY, c ^ dc))
        for x in range(NX)
        for y in range(NY)
        for c in range(NC)
    ]


def along(d):
    return cell_perm((d, 0), (0, d))


def across(d):
    return cell_perm((0, d), (d, 0))


SWAP = cell_perm((0, 0), (0, 0), 1)


def dp_perm(dz):
    return [(z, (z + dz) % NZ) for z in range(NZ)]


def place():
    me = lax.axis_index("cell")
    x, y, c = me // (NY * NC), (me // NC) % NY, me % NC
    first, second = jnp.where(c == 0, x, y), jnp.where(c == 0, y, x)
    return jnp.stack([first, second, c, lax.axis_index("dp")]).astype(I32)


def owner(c, first, second, oc):
    return jnp.where(c == 0, at(first, second, oc), at(second, first, oc))


def unit_owner(pos, d, rel, side):
    return owner(pos[2], lax.rem(pos[0] + d, 4), lax.rem(pos[1] + rel, 4), lax.rem(pos[2] + side, 2))


def gather_body(flows, head, pos, counts, vectors, *refs):
    header, refs = (refs[:2], refs[2:]) if head else ((), refs)
    outs = refs[: len(flows)]
    offsets, sems = refs[len(flows) : len(flows) + 2]
    total = jnp.int32(0)
    for o in range(OWNERS):
        offsets[o] = total
        total = total + counts[o]
    copies = []
    rows = RUN * ROWS // COPIES
    for out, (d, units) in zip(outs, flows):
        for i, (rel, side) in enumerate(units):
            start = jnp.minimum(offsets[unit_owner(pos, d, rel, side)], BLK - RUN)
            for part in range(COPIES):
                copies.append(
                    pltpu.make_async_copy(
                        vectors.at[pl.ds(pl.multiple_of(start * ROWS + part * rows, ROWS), rows)],
                        out.at[pl.ds((i * COPIES + part) * rows, rows)],
                        sems.at[len(copies)],
                    )
                )
                copies[-1].start()
    if head:
        cells, count_row = header
        text = refs[-1]
        text[...] = jnp.zeros((HEAD, D), F32)
        for i in range(BLK // D):
            text[i : i + 1, :] = cells[:, i * D : (i + 1) * D].astype(F32)
        text[BLK // D : BLK // D + 1, :OWNERS] = count_row[...].astype(F32)
        for out in outs:
            out[pl.ds(SLOTS * ROWS, HEAD), :] = text[...].astype(out.dtype)
    for copy in copies:
        copy.wait()


def gather_runs(flows, pos, counts, vectors, name, header=()):
    def body(*refs):
        gather_body(flows, bool(header), *refs)

    rows = SLOTS * ROWS + (HEAD if header else 0)
    return pl.pallas_call(
        body,
        out_shape=[jax.ShapeDtypeStruct((rows, D), vectors.dtype)] * len(flows),
        in_specs=[SMEM_SPEC, SMEM_SPEC, HBM_SPEC] + [VMEM_SPEC] * len(header),
        out_specs=[VMEM_SPEC] * len(flows),
        scratch_shapes=[pltpu.SMEM((OWNERS,), I32), pltpu.SemaphoreType.DMA((2 * COPIES * len(flows),))]
        + ([pltpu.VMEM((HEAD, D), F32)] if header else []),
        compiler_params=pltpu.CompilerParams(vmem_limit_bytes=LARGE_VMEM if header else SMALL_VMEM),
        name=name,
    )(pos, counts, vectors, *header)


def lists_body(pos, own_cells, own_counts, *refs):
    heads = refs[: GROUPS - 1]
    lists, sizes, tallies, offsets, text, metas, sem = refs[GROUPS - 1 :]
    for g, head in enumerate(heads):
        text[pl.ds(g * 8, 8), :] = head[...].astype(F32)[:8].astype(I32)
    copy = pltpu.make_async_copy(text, metas, sem.at[0])
    copy.start()

    def clear(i, _):
        for u in range(8):
            tallies[i * 8 + u] = jnp.int32(0)
        return 0

    lax.fori_loop(0, 4 * CHIP_CELLS // 8, clear, 0)
    copy.wait()

    def count_of(g, o):
        return own_counts[o] if g == 0 else metas[(g - 1) * 8 + BLK // D, o]

    def cell_of(g, i):
        return own_cells[i] if g == 0 else metas[(g - 1) * 8 + (i >> 7), i & (D - 1)]

    for g in range(GROUPS):
        total = jnp.int32(0)
        for o in range(OWNERS):
            offsets[g * OWNERS + o] = total
            total = total + count_of(g, o)
    begin = jnp.int32(0)
    for group, units in enumerate(UNITS):
        for g in range(GROUPS):
            filled = begin
            for i, (rel, side) in enumerate(units):
                o = unit_owner(pos, 0, rel, side)
                n = count_of(g, o)
                start = offsets[g * OWNERS + o]
                slot = i * RUN + start - jnp.minimum(start, BLK - RUN)
                base = (slot << 17) + i * ((PIECE // 8 << 7) + CELL_DEV)
                tally = group * CHIP_CELLS + i * CELL_DEV

                def add(j, f, g=g, start=start, base=base, tally=tally):
                    cell = cell_of(g, start + j)
                    lists[f + j] = base + (j << 17) + cell * ((ROWS // 8 << 7) + 1)
                    tallies[tally + cell] = tallies[tally + cell] + ROWS
                    return f

                lax.fori_loop(0, n, add, filled)
                filled = filled + n
            for j in range(PAIR):
                lists[filled + j] = jnp.int32((PACKED // 8 << 7) + CHIP_CELLS)
            segment = group * GROUPS + g
            sizes[2 * segment] = begin
            sizes[2 * segment + 1] = (filled - begin + PAIR - 1) // PAIR
            begin = begin + sizes[2 * segment + 1] * PAIR


def make_lists(pos, own_cells, own_counts, arrived):
    head = pl.BlockSpec((HEAD, D), lambda i: (SLOTS * ROWS // HEAD, 0))
    return pl.pallas_call(
        lists_body,
        out_shape=[
            jax.ShapeDtypeStruct((LIST,), I32),
            jax.ShapeDtypeStruct((8 * GROUPS,), I32),
            jax.ShapeDtypeStruct((4 * CHIP_CELLS,), I32),
        ],
        grid=(1,),
        in_specs=[SMEM_SPEC] * 3 + [head] * (GROUPS - 1),
        out_specs=[SMEM_SPEC] * 3,
        scratch_shapes=[
            pltpu.SMEM((GROUPS * OWNERS,), I32),
            pltpu.VMEM(((GROUPS - 1) * 8, D), I32),
            pltpu.SMEM(((GROUPS - 1) * 8, D), I32),
            pltpu.SemaphoreType.DMA((1,)),
        ],
        compiler_params=pltpu.CompilerParams(vmem_limit_bytes=SMALL_VMEM),
        name="lists",
    )(pos, own_cells, own_counts, *arrived)


def add_blocks(segment, lists, sizes, buf, acc, acc_s, acc_q):
    begin, steps = sizes[2 * segment], sizes[2 * segment + 1]
    row = lax.broadcasted_iota(I32, (ROWS, D), 0)
    lane = lax.broadcasted_iota(I32, (ROWS, D), 1)
    upper = lane >= row
    contract = (((0,), (0,)), ((), ()))

    def step(i, _):
        done = []
        for u in range(PAIR):
            entry = lists[begin + i * PAIR + u]
            block = buf[pl.ds(pl.multiple_of((entry >> 17) * ROWS, ROWS), ROWS), :]
            turned = jnp.concatenate([block[:, ROWS:], block[:, :ROWS]], axis=1)
            top = lax.dot_general(block[:, :ROWS], block, contract, preferred_element_type=F32)
            low = lax.dot_general(block[:, ROWS:], turned, contract, preferred_element_type=F32)
            wide = block.astype(F32)
            done.append(
                (
                    pl.multiple_of(((entry >> 7) & 1023) * 8, 8),
                    pl.multiple_of((entry & 127) * 8, 8),
                    jnp.where(upper, top, low),
                    jnp.sum(wide.reshape(8, 8, D), axis=0),
                    jnp.sum((wide * wide).reshape(8, 8, D), axis=0),
                )
            )
        for at_row, at_sum, gram, total, square in done:
            here, near = pl.ds(at_row, ROWS), pl.ds(at_sum, 8)
            acc[here, :] = acc[here, :] + gram
            acc_s[near, :] = acc_s[near, :] + total
            acc_q[near, :] = acc_q[near, :] + square
        return 0

    lax.fori_loop(0, steps, step, 0)


def gram_body(group, members, counted, started, lists, sizes, tallies, *refs):
    blocks, refs = refs[: len(members)], refs[len(members) :]
    first, second = started
    starts = (refs[:first], refs[first : first + second])
    outs, (acc, acc_s, acc_q) = refs[first + second : -3], refs[-3:]

    def add_starts(value, u, rows):
        for start in starts[u]:
            value = value + start[rows, :]
        return value

    def clear(i, _):
        rows = pl.ds(pl.multiple_of(i * ROWS, ROWS), ROWS)
        for u in range(2):
            value = add_starts(jnp.zeros((ROWS, D), F32), u, rows)
            acc[pl.ds(pl.multiple_of(u * PIECE + i * ROWS, 8), ROWS), :] = value
        return 0

    lax.fori_loop(0, PACKED // ROWS, clear, 0)

    def clear_sums(i, _):
        acc_s[pl.ds(pl.multiple_of(i * 8, 8), 8), :] = jnp.zeros((8, D), F32)
        acc_q[pl.ds(pl.multiple_of(i * 8, 8), 8), :] = jnp.zeros((8, D), F32)
        return 0

    lax.fori_loop(0, CHIP_CELLS, clear_sums, 0)
    for g, member in zip(members, blocks):
        add_blocks(group * GROUPS + g, lists, sizes, member, acc, acc_s, acc_q)
    lane = lax.broadcasted_iota(I32, (CELL_DEV, D), 1)
    for u in range(2):
        totals = []
        for source in (acc_s, acc_q):
            total = source[pl.ds(u * CELL_DEV * 8, CELL_DEV, stride=8), :]
            for j in range(1, 8):
                total = total + source[pl.ds(u * CELL_DEV * 8 + j, CELL_DEV, stride=8), :]
            totals.append(total)
        count = jnp.zeros((CELL_DEV, D), F32)
        if counted:
            for j in range(CELL_DEV):
                value = tallies[group * CHIP_CELLS + u * CELL_DEV + j].astype(F32)
                acc_s[pl.ds(u * CELL_DEV * 8 + j, 1), :] = jnp.full((1, D), value, F32)
            count = acc_s[pl.ds(u * CELL_DEV * 8, CELL_DEV), :]
        totals[1] = jnp.where(lane < ROWS, count, totals[1])
        for k, total in enumerate(totals):
            rows = PACKED + k * CELL_DEV
            acc[pl.ds(u * PIECE + rows, CELL_DEV), :] = add_starts(total, u, pl.ds(rows, CELL_DEV))

    def copy_out(i, _):
        for u in range(2):
            outs[u][pl.ds(pl.multiple_of(i * 32, 32), 32), :] = acc[
                pl.ds(pl.multiple_of(u * PIECE + i * 32, 32), 32), :
            ]
        return 0

    lax.fori_loop(0, PIECE // 32, copy_out, 0)


def gram(group, lists, sizes, tallies, blocks, first=(), second=(), members=(0, 1, 2, 3), counted=True):
    def body(*refs):
        gram_body(group, members, counted, (len(first), len(second)), *refs)

    half = jax.ShapeDtypeStruct((PIECE, D), F32)
    outs = [half] * 2
    return pl.pallas_call(
        body,
        out_shape=outs,
        in_specs=[SMEM_SPEC] * 3 + [VMEM_SPEC] * (len(members) + len(first) + len(second)),
        out_specs=[VMEM_SPEC] * len(outs),
        scratch_shapes=[pltpu.VMEM((NC * PIECE, D), F32)] + [pltpu.VMEM(((CHIP_CELLS + 1) * 8, D), F32)] * 2,
        compiler_params=pltpu.CompilerParams(vmem_limit_bytes=SMALL_VMEM),
        cost_estimate=pl.CostEstimate(flops=10**9, bytes_accessed=10**7, transcendentals=0),
        name=f"gram{group}" + ("" if counted else "b"),
    )(lists, sizes, tallies, *(blocks[g] for g in members), *first, *second)


def total_body(*refs):
    def step(i, _):
        rows = pl.ds(pl.multiple_of(i * 32, 32), 32)
        value = refs[0][rows, :]
        for part in refs[1:-1]:
            value = value + part[rows, :]
        refs[-1][rows, :] = value
        return 0

    lax.fori_loop(0, PIECE // 32, step, 0)


def other_total(parts):
    return pl.pallas_call(
        total_body,
        out_shape=jax.ShapeDtypeStruct((PIECE, D), F32),
        in_specs=[VMEM_SPEC] * len(parts),
        out_specs=VMEM_SPEC,
        compiler_params=pltpu.CompilerParams(vmem_limit_bytes=SMALL_VMEM),
        name="other_total",
    )(*parts)


def join_body(pos, *refs):
    outs, parts = refs[-NZ:], refs[:-NZ]
    z = pos[3]

    def total(rows):
        value = parts[0][rows, :]
        for part in parts[1:]:
            value = value + part[rows, :]
        return value

    for dz in range(NZ):
        q = lax.rem(z + dz, NZ)

        def put(rows, value, dz=dz):
            outs[dz][rows, :] = value

        def step(i, _, q=q, put=put):
            put(
                pl.ds(pl.multiple_of(i * ROWS, ROWS), ROWS),
                total(pl.ds(pl.multiple_of(q * QPACKED + i * ROWS, ROWS), ROWS)),
            )
            return 0

        lax.fori_loop(0, QCELL, step, 0)
        for k in range(2):
            put(
                pl.ds(QPACKED + k * QCELL, QCELL),
                total(pl.ds(pl.multiple_of(PACKED + k * CELL_DEV + q * QCELL, QCELL), QCELL)),
            )


def join(pos, parts):
    return pl.pallas_call(
        join_body,
        out_shape=[jax.ShapeDtypeStruct((QPIECE, D), F32)] * NZ,
        in_specs=[SMEM_SPEC] + [VMEM_SPEC] * len(parts),
        out_specs=[VMEM_SPEC] * NZ,
        compiler_params=pltpu.CompilerParams(vmem_limit_bytes=SMALL_VMEM),
        name="join",
    )(pos, *parts)


def finish_body(pos, *refs):
    parts = refs[:NZ]
    mean_out, cov_out = refs[NZ:]
    z = pos[3]
    row = lax.broadcasted_iota(I32, (ROWS, D), 0)
    lane = lax.broadcasted_iota(I32, (ROWS, D), 1)
    for dz in range(NZ):
        q = lax.rem(z + NZ - dz, NZ)
        part = parts[dz]
        sums = part[pl.ds(QPACKED, QCELL), :]
        counts = part[pl.ds(QPACKED + QCELL, QCELL), :]
        counts = jnp.where(lane[:QCELL] < ROWS, counts, pltpu.roll(counts, ROWS, 1))
        safe = jnp.maximum(counts, 1.0)
        mean = sums / safe
        inverse = jnp.where(counts > 0.0, 1.0 / safe, 0.0)
        mean_out[pl.ds(pl.multiple_of(q * QCELL, QCELL), QCELL), :] = mean
        scaled = jnp.transpose(jnp.concatenate([mean * counts] * (D // QCELL), axis=0))
        for j in range(QCELL):
            packed = part[pl.ds(j * ROWS, ROWS), :]
            diagonal = part[pl.ds(QPACKED + QCELL + j, 1), :]
            flipped = jnp.transpose(jnp.concatenate([packed, packed], axis=0))
            rolled = pltpu.roll(packed, ROWS, 1)
            high, low = flipped[:ROWS], flipped[ROWS:]
            top = jnp.where(lane >= row, packed, high)
            corner = jnp.where(lane - ROWS < row, rolled, jnp.where(lane - ROWS == row, diagonal, high))
            bottom = jnp.where(lane < ROWS, low, corner)
            full = jnp.concatenate([top, bottom], axis=0)
            outer = scaled[:, j : j + 1] * mean[j : j + 1, :]
            cov_out[q * QCELL + j] = (full - outer) * inverse[j : j + 1, :]


def finish(pos, parts):
    return pl.pallas_call(
        finish_body,
        out_shape=[
            jax.ShapeDtypeStruct((CELL_DEV, D), F32),
            jax.ShapeDtypeStruct((CELL_DEV, D, D), F32),
        ],
        in_specs=[SMEM_SPEC] + [VMEM_SPEC] * NZ,
        out_specs=[VMEM_SPEC, VMEM_SPEC],
        compiler_params=pltpu.CompilerParams(vmem_limit_bytes=VMEM_LIMIT),
        name="finish",
    )(pos, *parts)


def local(vectors, block_cells, dest_counts):
    pos = place()
    counts, cells = dest_counts[0, 0], block_cells[0]
    rows = pltpu.with_memory_space_constraint(vectors.reshape(BLK * ROWS, D), pltpu.HBM)
    sent, got = [], []
    for group, units in enumerate(UNITS):
        turn, flows, header = pos, [(d, units) for d in SHIFTS], ()
        if group == 0:
            flows, header = flows[1:], (block_cells, dest_counts[0])
        elif group == 1:
            turn, *_ = lax.optimization_barrier((pos, *sent[0]))
            flows = flows[1:]
        else:
            if group == 2:
                lists, sizes, tallies = make_lists(pos, cells, counts, got[0])
            turn, *_ = lax.optimization_barrier((pos, sizes, *got[group - 2][-3:]))
            flows = [(0, UNITS[group - 2])] + flows
        runs = gather_runs(flows, turn, counts, rows, f"gather{group}", header)
        sent.append(runs)
        if group > 1:
            got[group - 2].insert(0, runs[0])
        got.append(list(runs[1:-3]) + [lax.ppermute(run, "cell", along(d)) for d, run in zip(SHIFTS[1:], runs[-3:])])

    def step(rel, piece):
        return lax.ppermute(piece, "cell", across(rel))

    def grams(group, *rest, **options):
        return gram(group, lists, sizes, tallies, got[group], *rest, **options)

    fore, back = grams(0)
    fore, back = step(1, fore), step(3, back)
    left, right = grams(2)
    other1, own3 = step(1, left), step(3, right)
    left, right = grams(3, (fore,), (back,), members=(0, 1))
    left, right = grams(3, (left,), (right,), members=(2, 3), counted=False)
    own1, other3 = step(1, left), step(3, right)
    own, other = grams(1, (own3,), (other1,))
    swapped = lax.ppermute(other_total([other, other3]), "cell", SWAP)
    quarters = join(pos, [own, own1, swapped])
    mine = quarters[0]
    for dz in Z_SHIFTS:
        mine = mine + lax.ppermute(quarters[dz], "dp", dp_perm(dz))
    whole = {dz: lax.ppermute(mine, "dp", dp_perm(dz)) for dz in Z_SHIFTS}
    whole = [mine] + [whole[dz] for dz in range(1, NZ)]
    return tuple(finish(pos, whole))


def solution(mesh):
    in_specs = (P("dp", "cell", None, None), P("dp", "cell"), P("dp", "cell", None))
    out_specs = (P("cell", None), P("cell", None, None))
    return jax.shard_map(local, mesh=mesh, in_specs=in_specs, out_specs=out_specs, check_vma=False)
```

```python
import jax
import jax.numpy as jnp
from jax import lax
from jax.experimental import pallas as pl
from jax.experimental.pallas import tpu as pltpu
from jax.sharding import PartitionSpec as P

CELLS = 1024
NX = NY = NZ = 4
NC = 2
OWNERS = NX * NY * NC
CELL_DEV = CELLS // OWNERS
BLK = 384
ROWS = 64
D = 128
RUN = 24
SLOTS = NC * RUN
SHIFTS = (0, 1, 3, 2)
Z_SHIFTS = (1, 3, 2)
COPIES = 1
GROUPS = len(SHIFTS)
CHIP_CELLS = NC * CELL_DEV
LIST = 4 * GROUPS * SLOTS + 128
PAIR = 8
F32 = jnp.float32
I32 = jnp.int32
HEAD = 16
UNITS = (((2, 0), (2, 1)), ((0, 0), (0, 1)), ((1, 1), (3, 0)), ((1, 0), (3, 1)))
PACKED = (CELL_DEV - 1) * ROWS
PIECE = PACKED + 2 * CELL_DEV
QCELL = CELL_DEV // NZ
QPACKED = QCELL * ROWS
QPIECE = QPACKED + 2 * QCELL
VMEM_LIMIT = 16 * 1024 * 1024
LARGE_VMEM = 56 * 1024 * 1024
SMALL_VMEM = 6 * 1024 * 1024

SMEM_SPEC = pl.BlockSpec(memory_space=pltpu.SMEM)
VMEM_SPEC = pl.BlockSpec(memory_space=pltpu.VMEM)
HBM_SPEC = pl.BlockSpec(memory_space=pltpu.HBM)


def at(x, y, c):
    return (x * NY + y) * NC + c


def cell_perm(even, odd, dc=0):
    steps = (even, odd)
    return [
        (at(x, y, c), at((x + steps[c][0]) % NX, (y + steps[c][1]) % NY, c ^ dc))
        for x in range(NX)
        for y in range(NY)
        for c in range(NC)
    ]


def along(d):
    return cell_perm((d, 0), (0, d))


def across(d):
    return cell_perm((0, d), (d, 0))


SWAP = cell_perm((0, 0), (0, 0), 1)


def dp_perm(dz):
    return [(z, (z + dz) % NZ) for z in range(NZ)]


def place():
    me = lax.axis_index("cell")
    x, y, c = me // (NY * NC), (me // NC) % NY, me % NC
    first, second = jnp.where(c == 0, x, y), jnp.where(c == 0, y, x)
    return jnp.stack([first, second, c, lax.axis_index("dp")]).astype(I32)


def owner(c, first, second, oc):
    return jnp.where(c == 0, at(first, second, oc), at(second, first, oc))


def unit_owner(pos, d, rel, side):
    return owner(pos[2], lax.rem(pos[0] + d, 4), lax.rem(pos[1] + rel, 4), lax.rem(pos[2] + side, 2))


def gather_body(flows, head, pos, counts, vectors, *refs):
    header, refs = (refs[:2], refs[2:]) if head else ((), refs)
    outs = refs[: len(flows)]
    offsets, sems = refs[len(flows) : len(flows) + 2]
    total = jnp.int32(0)
    for o in range(OWNERS):
        offsets[o] = total
        total = total + counts[o]
    copies = []
    rows = RUN * ROWS // COPIES
    for out, (d, units) in zip(outs, flows):
        for i, (rel, side) in enumerate(units):
            start = jnp.minimum(offsets[unit_owner(pos, d, rel, side)], BLK - RUN)
            for part in range(COPIES):
                copies.append(
                    pltpu.make_async_copy(
                        vectors.at[pl.ds(pl.multiple_of(start * ROWS + part * rows, ROWS), rows)],
                        out.at[pl.ds((i * COPIES + part) * rows, rows)],
                        sems.at[len(copies)],
                    )
                )
                copies[-1].start()
    if head:
        cells, count_row = header
        text = refs[-1]
        text[...] = jnp.zeros((HEAD, D), F32)
        for i in range(BLK // D):
            text[i : i + 1, :] = cells[:, i * D : (i + 1) * D].astype(F32)
        text[BLK // D : BLK // D + 1, :OWNERS] = count_row[...].astype(F32)
        for out in outs:
            out[pl.ds(SLOTS * ROWS, HEAD), :] = text[...].astype(out.dtype)
    for copy in copies:
        copy.wait()


def gather_runs(flows, pos, counts, vectors, name, header=()):
    def body(*refs):
        gather_body(flows, bool(header), *refs)

    rows = SLOTS * ROWS + (HEAD if header else 0)
    return pl.pallas_call(
        body,
        out_shape=[jax.ShapeDtypeStruct((rows, D), vectors.dtype)] * len(flows),
        in_specs=[SMEM_SPEC, SMEM_SPEC, HBM_SPEC] + [VMEM_SPEC] * len(header),
        out_specs=[VMEM_SPEC] * len(flows),
        scratch_shapes=[pltpu.SMEM((OWNERS,), I32), pltpu.SemaphoreType.DMA((2 * COPIES * len(flows),))]
        + ([pltpu.VMEM((HEAD, D), F32)] if header else []),
        compiler_params=pltpu.CompilerParams(vmem_limit_bytes=LARGE_VMEM if header else SMALL_VMEM),
        name=name,
    )(pos, counts, vectors, *header)


def lists_body(pos, own_cells, own_counts, *refs):
    heads = refs[: GROUPS - 1]
    lists, sizes, tallies, offsets, text, metas, sem = refs[GROUPS - 1 :]
    for g, head in enumerate(heads):
        text[pl.ds(g * 8, 8), :] = head[...].astype(F32)[:8].astype(I32)
    copy = pltpu.make_async_copy(text, metas, sem.at[0])
    copy.start()

    def clear(i, _):
        for u in range(8):
            tallies[i * 8 + u] = jnp.int32(0)
        return 0

    lax.fori_loop(0, 4 * CHIP_CELLS // 8, clear, 0)
    copy.wait()

    def count_of(g, o):
        return own_counts[o] if g == 0 else metas[(g - 1) * 8 + BLK // D, o]

    def cell_of(g, i):
        return own_cells[i] if g == 0 else metas[(g - 1) * 8 + (i >> 7), i & (D - 1)]

    for g in range(GROUPS):
        total = jnp.int32(0)
        for o in range(OWNERS):
            offsets[g * OWNERS + o] = total
            total = total + count_of(g, o)
    begin = jnp.int32(0)
    for group, units in enumerate(UNITS):
        for g in range(GROUPS):
            filled = begin
            for i, (rel, side) in enumerate(units):
                o = unit_owner(pos, 0, rel, side)
                n = count_of(g, o)
                start = offsets[g * OWNERS + o]
                slot = i * RUN + start - jnp.minimum(start, BLK - RUN)
                base = (slot << 17) + i * ((PIECE // 8 << 7) + CELL_DEV)
                tally = group * CHIP_CELLS + i * CELL_DEV

                def add(j, f, g=g, start=start, base=base, tally=tally):
                    cell = cell_of(g, start + j)
                    lists[f + j] = base + (j << 17) + cell * ((ROWS // 8 << 7) + 1)
                    tallies[tally + cell] = tallies[tally + cell] + ROWS
                    return f

                lax.fori_loop(0, n, add, filled)
                filled = filled + n
            for j in range(PAIR):
                lists[filled + j] = jnp.int32((PACKED // 8 << 7) + CHIP_CELLS)
            segment = group * GROUPS + g
            sizes[2 * segment] = begin
            sizes[2 * segment + 1] = (filled - begin + PAIR - 1) // PAIR
            begin = begin + sizes[2 * segment + 1] * PAIR


def make_lists(pos, own_cells, own_counts, arrived):
    head = pl.BlockSpec((HEAD, D), lambda i: (SLOTS * ROWS // HEAD, 0))
    return pl.pallas_call(
        lists_body,
        out_shape=[
            jax.ShapeDtypeStruct((LIST,), I32),
            jax.ShapeDtypeStruct((8 * GROUPS,), I32),
            jax.ShapeDtypeStruct((4 * CHIP_CELLS,), I32),
        ],
        grid=(1,),
        in_specs=[SMEM_SPEC] * 3 + [head] * (GROUPS - 1),
        out_specs=[SMEM_SPEC] * 3,
        scratch_shapes=[
            pltpu.SMEM((GROUPS * OWNERS,), I32),
            pltpu.VMEM(((GROUPS - 1) * 8, D), I32),
            pltpu.SMEM(((GROUPS - 1) * 8, D), I32),
            pltpu.SemaphoreType.DMA((1,)),
        ],
        compiler_params=pltpu.CompilerParams(vmem_limit_bytes=SMALL_VMEM),
        name="lists",
    )(pos, own_cells, own_counts, *arrived)


def add_blocks(segment, lists, sizes, buf, acc, acc_s, acc_q):
    begin, steps = sizes[2 * segment], sizes[2 * segment + 1]
    row = lax.broadcasted_iota(I32, (ROWS, D), 0)
    lane = lax.broadcasted_iota(I32, (ROWS, D), 1)
    upper = lane >= row
    contract = (((0,), (0,)), ((), ()))

    def step(i, _):
        done = []
        for u in range(PAIR):
            entry = lists[begin + i * PAIR + u]
            block = buf[pl.ds(pl.multiple_of((entry >> 17) * ROWS, ROWS), ROWS), :]
            turned = jnp.concatenate([block[:, ROWS:], block[:, :ROWS]], axis=1)
            top = lax.dot_general(block[:, :ROWS], block, contract, preferred_element_type=F32)
            low = lax.dot_general(block[:, ROWS:], turned, contract, preferred_element_type=F32)
            wide = block.astype(F32)
            done.append(
                (
                    pl.multiple_of(((entry >> 7) & 1023) * 8, 8),
                    pl.multiple_of((entry & 127) * 8, 8),
                    jnp.where(upper, top, low),
                    jnp.sum(wide.reshape(8, 8, D), axis=0),
                    jnp.sum((wide * wide).reshape(8, 8, D), axis=0),
                )
            )
        for at_row, at_sum, gram, total, square in done:
            here, near = pl.ds(at_row, ROWS), pl.ds(at_sum, 8)
            acc[here, :] = acc[here, :] + gram
            acc_s[near, :] = acc_s[near, :] + total
            acc_q[near, :] = acc_q[near, :] + square
        return 0

    lax.fori_loop(0, steps, step, 0)


def gram_body(group, members, counted, started, lists, sizes, tallies, *refs):
    blocks, refs = refs[: len(members)], refs[len(members) :]
    first, second = started
    starts = (refs[:first], refs[first : first + second])
    outs, (acc, acc_s, acc_q) = refs[first + second : -3], refs[-3:]

    def add_starts(value, u, rows):
        for start in starts[u]:
            value = value + start[rows, :]
        return value

    def clear(i, _):
        rows = pl.ds(pl.multiple_of(i * ROWS, ROWS), ROWS)
        for u in range(2):
            value = add_starts(jnp.zeros((ROWS, D), F32), u, rows)
            acc[pl.ds(pl.multiple_of(u * PIECE + i * ROWS, 8), ROWS), :] = value
        return 0

    lax.fori_loop(0, PACKED // ROWS, clear, 0)

    def clear_sums(i, _):
        acc_s[pl.ds(pl.multiple_of(i * 8, 8), 8), :] = jnp.zeros((8, D), F32)
        acc_q[pl.ds(pl.multiple_of(i * 8, 8), 8), :] = jnp.zeros((8, D), F32)
        return 0

    lax.fori_loop(0, CHIP_CELLS, clear_sums, 0)
    for g, member in zip(members, blocks):
        add_blocks(group * GROUPS + g, lists, sizes, member, acc, acc_s, acc_q)
    lane = lax.broadcasted_iota(I32, (CELL_DEV, D), 1)
    for u in range(2):
        totals = []
        for source in (acc_s, acc_q):
            total = source[pl.ds(u * CELL_DEV * 8, CELL_DEV, stride=8), :]
            for j in range(1, 8):
                total = total + source[pl.ds(u * CELL_DEV * 8 + j, CELL_DEV, stride=8), :]
            totals.append(total)
        count = jnp.zeros((CELL_DEV, D), F32)
        if counted:
            for j in range(CELL_DEV):
                value = tallies[group * CHIP_CELLS + u * CELL_DEV + j].astype(F32)
                acc_s[pl.ds(u * CELL_DEV * 8 + j, 1), :] = jnp.full((1, D), value, F32)
            count = acc_s[pl.ds(u * CELL_DEV * 8, CELL_DEV), :]
        totals[1] = jnp.where(lane < ROWS, count, totals[1])
        for k, total in enumerate(totals):
            rows = PACKED + k * CELL_DEV
            acc[pl.ds(u * PIECE + rows, CELL_DEV), :] = add_starts(total, u, pl.ds(rows, CELL_DEV))

    def copy_out(i, _):
        for u in range(2):
            outs[u][pl.ds(pl.multiple_of(i * 32, 32), 32), :] = acc[
                pl.ds(pl.multiple_of(u * PIECE + i * 32, 32), 32), :
            ]
        return 0

    lax.fori_loop(0, PIECE // 32, copy_out, 0)


def gram(group, lists, sizes, tallies, blocks, first=(), second=(), members=(0, 1, 2, 3), counted=True):
    def body(*refs):
        gram_body(group, members, counted, (len(first), len(second)), *refs)

    half = jax.ShapeDtypeStruct((PIECE, D), F32)
    outs = [half] * 2
    return pl.pallas_call(
        body,
        out_shape=outs,
        in_specs=[SMEM_SPEC] * 3 + [VMEM_SPEC] * (len(members) + len(first) + len(second)),
        out_specs=[VMEM_SPEC] * len(outs),
        scratch_shapes=[pltpu.VMEM((NC * PIECE, D), F32)] + [pltpu.VMEM(((CHIP_CELLS + 1) * 8, D), F32)] * 2,
        compiler_params=pltpu.CompilerParams(vmem_limit_bytes=SMALL_VMEM),
        cost_estimate=pl.CostEstimate(flops=10**9, bytes_accessed=10**7, transcendentals=0),
        name=f"gram{group}" + ("" if counted else "b"),
    )(lists, sizes, tallies, *(blocks[g] for g in members), *first, *second)


def total_body(*refs):
    def step(i, _):
        rows = pl.ds(pl.multiple_of(i * 32, 32), 32)
        value = refs[0][rows, :]
        for part in refs[1:-1]:
            value = value + part[rows, :]
        refs[-1][rows, :] = value
        return 0

    lax.fori_loop(0, PIECE // 32, step, 0)


def other_total(parts):
    return pl.pallas_call(
        total_body,
        out_shape=jax.ShapeDtypeStruct((PIECE, D), F32),
        in_specs=[VMEM_SPEC] * len(parts),
        out_specs=VMEM_SPEC,
        compiler_params=pltpu.CompilerParams(vmem_limit_bytes=SMALL_VMEM),
        name="other_total",
    )(*parts)


def join_body(pos, *refs):
    outs, parts = refs[-NZ:], refs[:-NZ]
    z = pos[3]

    def total(rows):
        value = parts[0][rows, :]
        for part in parts[1:]:
            value = value + part[rows, :]
        return value

    for dz in range(NZ):
        q = lax.rem(z + dz, NZ)

        def put(rows, value, dz=dz):
            outs[dz][rows, :] = value

        def step(i, _, q=q, put=put):
            put(
                pl.ds(pl.multiple_of(i * ROWS, ROWS), ROWS),
                total(pl.ds(pl.multiple_of(q * QPACKED + i * ROWS, ROWS), ROWS)),
            )
            return 0

        lax.fori_loop(0, QCELL, step, 0)
        for k in range(2):
            put(
                pl.ds(QPACKED + k * QCELL, QCELL),
                total(pl.ds(pl.multiple_of(PACKED + k * CELL_DEV + q * QCELL, QCELL), QCELL)),
            )


def join(pos, parts):
    return pl.pallas_call(
        join_body,
        out_shape=[jax.ShapeDtypeStruct((QPIECE, D), F32)] * NZ,
        in_specs=[SMEM_SPEC] + [VMEM_SPEC] * len(parts),
        out_specs=[VMEM_SPEC] * NZ,
        compiler_params=pltpu.CompilerParams(vmem_limit_bytes=SMALL_VMEM),
        name="join",
    )(pos, *parts)


def finish_body(pos, *refs):
    parts = refs[:NZ]
    mean_out, cov_out = refs[NZ:]
    z = pos[3]
    row = lax.broadcasted_iota(I32, (ROWS, D), 0)
    lane = lax.broadcasted_iota(I32, (ROWS, D), 1)
    for dz in range(NZ):
        q = lax.rem(z + NZ - dz, NZ)
        part = parts[dz]
        sums = part[pl.ds(QPACKED, QCELL), :]
        counts = part[pl.ds(QPACKED + QCELL, QCELL), :]
        counts = jnp.where(lane[:QCELL] < ROWS, counts, pltpu.roll(counts, ROWS, 1))
        safe = jnp.maximum(counts, 1.0)
        mean = sums / safe
        inverse = jnp.where(counts > 0.0, 1.0 / safe, 0.0)
        mean_out[pl.ds(pl.multiple_of(q * QCELL, QCELL), QCELL), :] = mean
        scaled = jnp.transpose(jnp.concatenate([mean * counts] * (D // QCELL), axis=0))
        for j in range(QCELL):
            packed = part[pl.ds(j * ROWS, ROWS), :]
            diagonal = part[pl.ds(QPACKED + QCELL + j, 1), :]
            flipped = jnp.transpose(jnp.concatenate([packed, packed], axis=0))
            rolled = pltpu.roll(packed, ROWS, 1)
            high, low = flipped[:ROWS], flipped[ROWS:]
            top = jnp.where(lane >= row, packed, high)
            corner = jnp.where(lane - ROWS < row, rolled, jnp.where(lane - ROWS == row, diagonal, high))
            bottom = jnp.where(lane < ROWS, low, corner)
            full = jnp.concatenate([top, bottom], axis=0)
            outer = scaled[:, j : j + 1] * mean[j : j + 1, :]
            cov_out[q * QCELL + j] = (full - outer) * inverse[j : j + 1, :]


def finish(pos, parts):
    return pl.pallas_call(
        finish_body,
        out_shape=[
            jax.ShapeDtypeStruct((CELL_DEV, D), F32),
            jax.ShapeDtypeStruct((CELL_DEV, D, D), F32),
        ],
        in_specs=[SMEM_SPEC] + [VMEM_SPEC] * NZ,
        out_specs=[VMEM_SPEC, VMEM_SPEC],
        compiler_params=pltpu.CompilerParams(vmem_limit_bytes=VMEM_LIMIT),
        name="finish",
    )(pos, *parts)


def local(vectors, block_cells, dest_counts):
    pos = place()
    counts, cells = dest_counts[0, 0], block_cells[0]
    rows = pltpu.with_memory_space_constraint(vectors.reshape(BLK * ROWS, D), pltpu.HBM)
    sent, got = [], []
    for group, units in enumerate(UNITS):
        turn, flows, header = pos, [(d, units) for d in SHIFTS], ()
        if group == 0:
            flows, header = flows[1:], (block_cells, dest_counts[0])
        elif group == 1:
            turn, *_ = lax.optimization_barrier((pos, *sent[0]))
            flows = flows[1:]
        else:
            if group == 2:
                lists, sizes, tallies = make_lists(pos, cells, counts, got[0])
            turn, *_ = lax.optimization_barrier((pos, sizes, *got[group - 2][-3:]))
            flows = [(0, UNITS[group - 2])] + flows
        runs = gather_runs(flows, turn, counts, rows, f"gather{group}", header)
        sent.append(runs)
        if group > 1:
            got[group - 2].insert(0, runs[0])
        got.append(list(runs[1:-3]) + [lax.ppermute(run, "cell", along(d)) for d, run in zip(SHIFTS[1:], runs[-3:])])

    def step(rel, piece):
        return lax.ppermute(piece, "cell", across(rel))

    def grams(group, *rest, **options):
        return gram(group, lists, sizes, tallies, got[group], *rest, **options)

    fore, back = grams(0)
    fore, back = step(1, fore), step(3, back)
    left, right = grams(2)
    other1, own3 = step(1, left), step(3, right)
    left, right = grams(3, (fore,), (back,), members=(0, 1, 2))
    left, right = grams(3, (left,), (right,), members=(3,), counted=False)
    own1, other3 = step(1, left), step(3, right)
    own, other = grams(1, (own3,), (other1,))
    swapped = lax.ppermute(other_total([other, other3]), "cell", SWAP)
    quarters = join(pos, [own, own1, swapped])
    mine = quarters[0]
    for dz in Z_SHIFTS:
        mine = mine + lax.ppermute(quarters[dz], "dp", dp_perm(dz))
    whole = {dz: lax.ppermute(mine, "dp", dp_perm(dz)) for dz in Z_SHIFTS}
    whole = [mine] + [whole[dz] for dz in range(1, NZ)]
    return tuple(finish(pos, whole))


def solution(mesh):
    in_specs = (P("dp", "cell", None, None), P("dp", "cell"), P("dp", "cell", None))
    out_specs = (P("cell", None), P("cell", None, None))
    return jax.shard_map(local, mesh=mesh, in_specs=in_specs, out_specs=out_specs, check_vma=False)
```

```python
import jax
import jax.numpy as jnp
from jax import lax
from jax.experimental import pallas as pl
from jax.experimental.pallas import tpu as pltpu
from jax.sharding import PartitionSpec as P

CELLS = 1024
NX = NY = NZ = 4
NC = 2
OWNERS = NX * NY * NC
CELL_DEV = CELLS // OWNERS
BLK = 384
ROWS = 64
D = 128
RUN = 24
SLOTS = NC * RUN
SHIFTS = (0, 1, 3, 2)
Z_SHIFTS = (1, 3, 2)
COPIES = 1
GROUPS = len(SHIFTS)
CHIP_CELLS = NC * CELL_DEV
LIST = 4 * GROUPS * SLOTS + 128
PAIR = 8
F32 = jnp.float32
I32 = jnp.int32
HEAD = 16
UNITS = (((2, 0), (2, 1)), ((0, 0), (0, 1)), ((1, 1), (3, 0)), ((1, 0), (3, 1)))
PACKED = (CELL_DEV - 1) * ROWS
PIECE = PACKED + 2 * CELL_DEV
QCELL = CELL_DEV // NZ
QPACKED = QCELL * ROWS
QPIECE = QPACKED + 2 * QCELL
VMEM_LIMIT = 16 * 1024 * 1024
LARGE_VMEM = 56 * 1024 * 1024
SMALL_VMEM = 6 * 1024 * 1024

SMEM_SPEC = pl.BlockSpec(memory_space=pltpu.SMEM)
VMEM_SPEC = pl.BlockSpec(memory_space=pltpu.VMEM)
HBM_SPEC = pl.BlockSpec(memory_space=pltpu.HBM)


def at(x, y, c):
    return (x * NY + y) * NC + c


def cell_perm(even, odd, dc=0):
    steps = (even, odd)
    return [
        (at(x, y, c), at((x + steps[c][0]) % NX, (y + steps[c][1]) % NY, c ^ dc))
        for x in range(NX)
        for y in range(NY)
        for c in range(NC)
    ]


def along(d):
    return cell_perm((d, 0), (0, d))


def across(d):
    return cell_perm((0, d), (d, 0))


SWAP = cell_perm((0, 0), (0, 0), 1)


def dp_perm(dz):
    return [(z, (z + dz) % NZ) for z in range(NZ)]


def place():
    me = lax.axis_index("cell")
    x, y, c = me // (NY * NC), (me // NC) % NY, me % NC
    first, second = jnp.where(c == 0, x, y), jnp.where(c == 0, y, x)
    return jnp.stack([first, second, c, lax.axis_index("dp")]).astype(I32)


def owner(c, first, second, oc):
    return jnp.where(c == 0, at(first, second, oc), at(second, first, oc))


def unit_owner(pos, d, rel, side):
    return owner(pos[2], lax.rem(pos[0] + d, 4), lax.rem(pos[1] + rel, 4), lax.rem(pos[2] + side, 2))


def gather_body(flows, head, pos, counts, vectors, *refs):
    header, refs = (refs[:2], refs[2:]) if head else ((), refs)
    outs = refs[: len(flows)]
    offsets, sems = refs[len(flows) : len(flows) + 2]
    total = jnp.int32(0)
    for o in range(OWNERS):
        offsets[o] = total
        total = total + counts[o]
    copies = []
    rows = RUN * ROWS // COPIES
    for out, (d, units) in zip(outs, flows):
        for i, (rel, side) in enumerate(units):
            start = jnp.minimum(offsets[unit_owner(pos, d, rel, side)], BLK - RUN)
            for part in range(COPIES):
                copies.append(
                    pltpu.make_async_copy(
                        vectors.at[pl.ds(pl.multiple_of(start * ROWS + part * rows, ROWS), rows)],
                        out.at[pl.ds((i * COPIES + part) * rows, rows)],
                        sems.at[len(copies)],
                    )
                )
                copies[-1].start()
    if head:
        cells, count_row = header
        text = refs[-1]
        text[...] = jnp.zeros((HEAD, D), F32)
        for i in range(BLK // D):
            text[i : i + 1, :] = cells[:, i * D : (i + 1) * D].astype(F32)
        text[BLK // D : BLK // D + 1, :OWNERS] = count_row[...].astype(F32)
        for out in outs:
            out[pl.ds(SLOTS * ROWS, HEAD), :] = text[...].astype(out.dtype)
    for copy in copies:
        copy.wait()


def gather_runs(flows, pos, counts, vectors, name, header=()):
    def body(*refs):
        gather_body(flows, bool(header), *refs)

    rows = SLOTS * ROWS + (HEAD if header else 0)
    return pl.pallas_call(
        body,
        out_shape=[jax.ShapeDtypeStruct((rows, D), vectors.dtype)] * len(flows),
        in_specs=[SMEM_SPEC, SMEM_SPEC, HBM_SPEC] + [VMEM_SPEC] * len(header),
        out_specs=[VMEM_SPEC] * len(flows),
        scratch_shapes=[pltpu.SMEM((OWNERS,), I32), pltpu.SemaphoreType.DMA((2 * COPIES * len(flows),))]
        + ([pltpu.VMEM((HEAD, D), F32)] if header else []),
        compiler_params=pltpu.CompilerParams(vmem_limit_bytes=LARGE_VMEM if header else SMALL_VMEM),
        name=name,
    )(pos, counts, vectors, *header)


def lists_body(pos, own_cells, own_counts, *refs):
    heads = refs[: GROUPS - 1]
    lists, sizes, tallies, offsets, text, metas, sem = refs[GROUPS - 1 :]
    for g, head in enumerate(heads):
        text[pl.ds(g * 8, 8), :] = head[...].astype(F32)[:8].astype(I32)
    copy = pltpu.make_async_copy(text, metas, sem.at[0])
    copy.start()

    def clear(i, _):
        for u in range(8):
            tallies[i * 8 + u] = jnp.int32(0)
        return 0

    lax.fori_loop(0, 4 * CHIP_CELLS // 8, clear, 0)
    copy.wait()

    def count_of(g, o):
        return own_counts[o] if g == 0 else metas[(g - 1) * 8 + BLK // D, o]

    def cell_of(g, i):
        return own_cells[i] if g == 0 else metas[(g - 1) * 8 + (i >> 7), i & (D - 1)]

    for g in range(GROUPS):
        total = jnp.int32(0)
        for o in range(OWNERS):
            offsets[g * OWNERS + o] = total
            total = total + count_of(g, o)
    begin = jnp.int32(0)
    for group, units in enumerate(UNITS):
        for g in range(GROUPS):
            filled = begin
            for i, (rel, side) in enumerate(units):
                o = unit_owner(pos, 0, rel, side)
                n = count_of(g, o)
                start = offsets[g * OWNERS + o]
                slot = i * RUN + start - jnp.minimum(start, BLK - RUN)
                base = (slot << 17) + i * ((PIECE // 8 << 7) + CELL_DEV)
                tally = group * CHIP_CELLS + i * CELL_DEV

                def add(j, f, g=g, start=start, base=base, tally=tally):
                    cell = cell_of(g, start + j)
                    lists[f + j] = base + (j << 17) + cell * ((ROWS // 8 << 7) + 1)
                    tallies[tally + cell] = tallies[tally + cell] + ROWS
                    return f

                lax.fori_loop(0, n, add, filled)
                filled = filled + n
            for j in range(PAIR):
                lists[filled + j] = jnp.int32((PACKED // 8 << 7) + CHIP_CELLS)
            segment = group * GROUPS + g
            sizes[2 * segment] = begin
            sizes[2 * segment + 1] = (filled - begin + PAIR - 1) // PAIR
            begin = begin + sizes[2 * segment + 1] * PAIR


def make_lists(pos, own_cells, own_counts, arrived):
    head = pl.BlockSpec((HEAD, D), lambda i: (SLOTS * ROWS // HEAD, 0))
    return pl.pallas_call(
        lists_body,
        out_shape=[
            jax.ShapeDtypeStruct((LIST,), I32),
            jax.ShapeDtypeStruct((8 * GROUPS,), I32),
            jax.ShapeDtypeStruct((4 * CHIP_CELLS,), I32),
        ],
        grid=(1,),
        in_specs=[SMEM_SPEC] * 3 + [head] * (GROUPS - 1),
        out_specs=[SMEM_SPEC] * 3,
        scratch_shapes=[
            pltpu.SMEM((GROUPS * OWNERS,), I32),
            pltpu.VMEM(((GROUPS - 1) * 8, D), I32),
            pltpu.SMEM(((GROUPS - 1) * 8, D), I32),
            pltpu.SemaphoreType.DMA((1,)),
        ],
        compiler_params=pltpu.CompilerParams(vmem_limit_bytes=SMALL_VMEM),
        name="lists",
    )(pos, own_cells, own_counts, *arrived)


def add_blocks(segment, lists, sizes, buf, acc, acc_s, acc_q):
    begin, steps = sizes[2 * segment], sizes[2 * segment + 1]
    row = lax.broadcasted_iota(I32, (ROWS, D), 0)
    lane = lax.broadcasted_iota(I32, (ROWS, D), 1)
    upper = lane >= row
    contract = (((0,), (0,)), ((), ()))

    def step(i, _):
        done = []
        for u in range(PAIR):
            entry = lists[begin + i * PAIR + u]
            block = buf[pl.ds(pl.multiple_of((entry >> 17) * ROWS, ROWS), ROWS), :]
            turned = jnp.concatenate([block[:, ROWS:], block[:, :ROWS]], axis=1)
            top = lax.dot_general(block[:, :ROWS], block, contract, preferred_element_type=F32)
            low = lax.dot_general(block[:, ROWS:], turned, contract, preferred_element_type=F32)
            wide = block.astype(F32)
            done.append(
                (
                    pl.multiple_of(((entry >> 7) & 1023) * 8, 8),
                    pl.multiple_of((entry & 127) * 8, 8),
                    jnp.where(upper, top, low),
                    jnp.sum(wide.reshape(8, 8, D), axis=0),
                    jnp.sum((wide * wide).reshape(8, 8, D), axis=0),
                )
            )
        for at_row, at_sum, gram, total, square in done:
            here, near = pl.ds(at_row, ROWS), pl.ds(at_sum, 8)
            acc[here, :] = acc[here, :] + gram
            acc_s[near, :] = acc_s[near, :] + total
            acc_q[near, :] = acc_q[near, :] + square
        return 0

    lax.fori_loop(0, steps, step, 0)


def gram_body(group, members, counted, started, lists, sizes, tallies, *refs):
    blocks, refs = refs[: len(members)], refs[len(members) :]
    first, second = started
    starts = (refs[:first], refs[first : first + second])
    outs, (acc, acc_s, acc_q) = refs[first + second : -3], refs[-3:]

    def add_starts(value, u, rows):
        for start in starts[u]:
            value = value + start[rows, :]
        return value

    def clear(i, _):
        rows = pl.ds(pl.multiple_of(i * ROWS, ROWS), ROWS)
        for u in range(2):
            value = add_starts(jnp.zeros((ROWS, D), F32), u, rows)
            acc[pl.ds(pl.multiple_of(u * PIECE + i * ROWS, 8), ROWS), :] = value
        return 0

    lax.fori_loop(0, PACKED // ROWS, clear, 0)

    def clear_sums(i, _):
        acc_s[pl.ds(pl.multiple_of(i * 8, 8), 8), :] = jnp.zeros((8, D), F32)
        acc_q[pl.ds(pl.multiple_of(i * 8, 8), 8), :] = jnp.zeros((8, D), F32)
        return 0

    lax.fori_loop(0, CHIP_CELLS, clear_sums, 0)
    for g, member in zip(members, blocks):
        add_blocks(group * GROUPS + g, lists, sizes, member, acc, acc_s, acc_q)
    lane = lax.broadcasted_iota(I32, (CELL_DEV, D), 1)
    for u in range(2):
        totals = []
        for source in (acc_s, acc_q):
            total = source[pl.ds(u * CELL_DEV * 8, CELL_DEV, stride=8), :]
            for j in range(1, 8):
                total = total + source[pl.ds(u * CELL_DEV * 8 + j, CELL_DEV, stride=8), :]
            totals.append(total)
        count = jnp.zeros((CELL_DEV, D), F32)
        if counted:
            for j in range(CELL_DEV):
                value = tallies[group * CHIP_CELLS + u * CELL_DEV + j].astype(F32)
                acc_s[pl.ds(u * CELL_DEV * 8 + j, 1), :] = jnp.full((1, D), value, F32)
            count = acc_s[pl.ds(u * CELL_DEV * 8, CELL_DEV), :]
        totals[1] = jnp.where(lane < ROWS, count, totals[1])
        for k, total in enumerate(totals):
            rows = PACKED + k * CELL_DEV
            acc[pl.ds(u * PIECE + rows, CELL_DEV), :] = add_starts(total, u, pl.ds(rows, CELL_DEV))

    def copy_out(i, _):
        for u in range(2):
            outs[u][pl.ds(pl.multiple_of(i * 32, 32), 32), :] = acc[
                pl.ds(pl.multiple_of(u * PIECE + i * 32, 32), 32), :
            ]
        return 0

    lax.fori_loop(0, PIECE // 32, copy_out, 0)


def gram(group, lists, sizes, tallies, blocks, first=(), second=(), members=(0, 1, 2, 3), counted=True):
    def body(*refs):
        gram_body(group, members, counted, (len(first), len(second)), *refs)

    half = jax.ShapeDtypeStruct((PIECE, D), F32)
    outs = [half] * 2
    return pl.pallas_call(
        body,
        out_shape=outs,
        in_specs=[SMEM_SPEC] * 3 + [VMEM_SPEC] * (len(members) + len(first) + len(second)),
        out_specs=[VMEM_SPEC] * len(outs),
        scratch_shapes=[pltpu.VMEM((NC * PIECE, D), F32)] + [pltpu.VMEM(((CHIP_CELLS + 1) * 8, D), F32)] * 2,
        compiler_params=pltpu.CompilerParams(vmem_limit_bytes=SMALL_VMEM),
        cost_estimate=pl.CostEstimate(flops=10**9, bytes_accessed=10**7, transcendentals=0),
        name=f"gram{group}" + ("" if counted else "b"),
    )(lists, sizes, tallies, *(blocks[g] for g in members), *first, *second)


def total_body(*refs):
    def step(i, _):
        rows = pl.ds(pl.multiple_of(i * 32, 32), 32)
        value = refs[0][rows, :]
        for part in refs[1:-1]:
            value = value + part[rows, :]
        refs[-1][rows, :] = value
        return 0

    lax.fori_loop(0, PIECE // 32, step, 0)


def other_total(parts):
    return pl.pallas_call(
        total_body,
        out_shape=jax.ShapeDtypeStruct((PIECE, D), F32),
        in_specs=[VMEM_SPEC] * len(parts),
        out_specs=VMEM_SPEC,
        compiler_params=pltpu.CompilerParams(vmem_limit_bytes=SMALL_VMEM),
        name="other_total",
    )(*parts)


def join_body(pos, *refs):
    outs, parts = refs[-NZ:], refs[:-NZ]
    z = pos[3]

    def total(rows):
        value = parts[0][rows, :]
        for part in parts[1:]:
            value = value + part[rows, :]
        return value

    for dz in range(NZ):
        q = lax.rem(z + dz, NZ)

        def put(rows, value, dz=dz):
            outs[dz][rows, :] = value

        def step(i, _, q=q, put=put):
            put(
                pl.ds(pl.multiple_of(i * ROWS, ROWS), ROWS),
                total(pl.ds(pl.multiple_of(q * QPACKED + i * ROWS, ROWS), ROWS)),
            )
            return 0

        lax.fori_loop(0, QCELL, step, 0)
        for k in range(2):
            put(
                pl.ds(QPACKED + k * QCELL, QCELL),
                total(pl.ds(pl.multiple_of(PACKED + k * CELL_DEV + q * QCELL, QCELL), QCELL)),
            )


def join(pos, parts):
    return pl.pallas_call(
        join_body,
        out_shape=[jax.ShapeDtypeStruct((QPIECE, D), F32)] * NZ,
        in_specs=[SMEM_SPEC] + [VMEM_SPEC] * len(parts),
        out_specs=[VMEM_SPEC] * NZ,
        compiler_params=pltpu.CompilerParams(vmem_limit_bytes=SMALL_VMEM),
        name="join",
    )(pos, *parts)


def finish_body(pos, *refs):
    parts = refs[:NZ]
    mean_out, cov_out = refs[NZ:]
    z = pos[3]
    row = lax.broadcasted_iota(I32, (ROWS, D), 0)
    lane = lax.broadcasted_iota(I32, (ROWS, D), 1)
    for dz in range(NZ):
        q = lax.rem(z + NZ - dz, NZ)
        part = parts[dz]
        sums = part[pl.ds(QPACKED, QCELL), :]
        counts = part[pl.ds(QPACKED + QCELL, QCELL), :]
        counts = jnp.where(lane[:QCELL] < ROWS, counts, pltpu.roll(counts, ROWS, 1))
        safe = jnp.maximum(counts, 1.0)
        mean = sums / safe
        inverse = jnp.where(counts > 0.0, 1.0 / safe, 0.0)
        mean_out[pl.ds(pl.multiple_of(q * QCELL, QCELL), QCELL), :] = mean
        scaled = jnp.transpose(jnp.concatenate([mean * counts] * (D // QCELL), axis=0))
        for j in range(QCELL):
            packed = part[pl.ds(j * ROWS, ROWS), :]
            diagonal = part[pl.ds(QPACKED + QCELL + j, 1), :]
            flipped = jnp.transpose(jnp.concatenate([packed, packed], axis=0))
            rolled = pltpu.roll(packed, ROWS, 1)
            high, low = flipped[:ROWS], flipped[ROWS:]
            top = jnp.where(lane >= row, packed, high)
            corner = jnp.where(lane - ROWS < row, rolled, jnp.where(lane - ROWS == row, diagonal, high))
            bottom = jnp.where(lane < ROWS, low, corner)
            full = jnp.concatenate([top, bottom], axis=0)
            outer = scaled[:, j : j + 1] * mean[j : j + 1, :]
            cov_out[q * QCELL + j] = (full - outer) * inverse[j : j + 1, :]


def finish(pos, parts):
    return pl.pallas_call(
        finish_body,
        out_shape=[
            jax.ShapeDtypeStruct((CELL_DEV, D), F32),
            jax.ShapeDtypeStruct((CELL_DEV, D, D), F32),
        ],
        in_specs=[SMEM_SPEC] + [VMEM_SPEC] * NZ,
        out_specs=[VMEM_SPEC, VMEM_SPEC],
        compiler_params=pltpu.CompilerParams(vmem_limit_bytes=VMEM_LIMIT),
        name="finish",
    )(pos, *parts)


def local(vectors, block_cells, dest_counts):
    pos = place()
    counts, cells = dest_counts[0, 0], block_cells[0]
    rows = pltpu.with_memory_space_constraint(vectors.reshape(BLK * ROWS, D), pltpu.HBM)
    sent, got = [], []
    for group, units in enumerate(UNITS):
        turn, flows, header = pos, [(d, units) for d in SHIFTS], ()
        if group == 0:
            flows, header = flows[1:], (block_cells, dest_counts[0])
        elif group == 1:
            turn, *_ = lax.optimization_barrier((pos, *sent[0]))
            flows = flows[1:]
        else:
            if group == 2:
                lists, sizes, tallies = make_lists(pos, cells, counts, got[0])
            turn, *_ = lax.optimization_barrier((pos, sizes, *got[group - 2][-3:]))
            flows = [(0, UNITS[group - 2])] + flows
        runs = gather_runs(flows, turn, counts, rows, f"gather{group}", header)
        sent.append(runs)
        if group > 1:
            got[group - 2].insert(0, runs[0])
        got.append(list(runs[1:-3]) + [lax.ppermute(run, "cell", along(d)) for d, run in zip(SHIFTS[1:], runs[-3:])])

    def step(rel, piece):
        return lax.ppermute(piece, "cell", across(rel))

    def grams(group, *rest, **options):
        return gram(group, lists, sizes, tallies, got[group], *rest, **options)

    fore, back = grams(0)
    fore, back = step(1, fore), step(3, back)
    left, right = grams(2, members=(0, 1, 2))
    left, right = grams(2, (left,), (right,), members=(3,), counted=False)
    other1, own3 = step(1, left), step(3, right)
    left, right = grams(3, (fore,), (back,), members=(0, 1, 2))
    left, right = grams(3, (left,), (right,), members=(3,), counted=False)
    own1, other3 = step(1, left), step(3, right)
    own, other = grams(1, (own3,), (other1,))
    swapped = lax.ppermute(other_total([other, other3]), "cell", SWAP)
    quarters = join(pos, [own, own1, swapped])
    mine = quarters[0]
    for dz in Z_SHIFTS:
        mine = mine + lax.ppermute(quarters[dz], "dp", dp_perm(dz))
    whole = {dz: lax.ppermute(mine, "dp", dp_perm(dz)) for dz in Z_SHIFTS}
    whole = [mine] + [whole[dz] for dz in range(1, NZ)]
    return tuple(finish(pos, whole))


def solution(mesh):
    in_specs = (P("dp", "cell", None, None), P("dp", "cell"), P("dp", "cell", None))
    out_specs = (P("cell", None), P("cell", None, None))
    return jax.shard_map(local, mesh=mesh, in_specs=in_specs, out_specs=out_specs, check_vma=False)
```
